256 devices in a mesh: row: 8 (over x, y_lo), col: 32 (over z, y_hi, core).
Axes of the slice: x: 4, y: 4 (y_hi: 2, y_lo: 2; y = y_hi * 2 + y_lo), z: 8, core: 2. Of those that a mesh axis runs over, the one named last changes fastest.
Arguments:
- raw_spectra: float32 [1280, 64, 2, 512], P(('row', 'col')), may hold values from -250 to 250, as said below
- seg_valid: int32 [1280, 64], P(('row', 'col')), may hold values 0 or 1
- slot_order: int32 [1280], P(('row', 'col')), may hold values from 0 to 4, as said below
Outputs:
- stacked: bfloat16 [1280, 1280, 512], P('row', 'col')
The draws below stay inside these ranges and needn't reach their ends.
Inputs may be any that keep to these rules, and one draw needn't show every extreme that they name: `raw_spectra`: spectra of noise segments; levels differ by channel, segment and frequency. `slot_order`: in each aligned block of 5 entries, a permutation of 0 to 4.
All inputs are finite; a program needn't handle non-finite values. No bound on the sum of `seg_valid` on one device may be relied on, other than what follows from the above.
Results may differ from the reference program's by a relative error of at most 0.0068.
Values may be sent and summed in bfloat16 or wider, within the bound.
No kernel may reach another device: no remote copies, remote signals or barrier semaphores. Data moves between devices by JAX's collectives and lax.ppermute only.
A program may use at most 192 MiB of HBM per device.

```python
import math
import jax
import jax.numpy as jnp
from jax import lax

CH_DEV = 5
SEG = 64
FREQ = 512
LAGS = 512
HALF_BAND = 64
CHANNELS = 1280
ROW_BLOCK = 160
N_ROW = 8
N_COL = 32


def draw_raw_spectra(key, part):
    keys = jax.random.split(jax.random.fold_in(key, 11), 5)
    shape = (CHANNELS, SEG, 2, FREQ)
    lead = (CHANNELS, SEG, 1, 1)
    rough = jnp.clip(jax.random.normal(keys[0], shape, jnp.float32), -5.0, 5.0)
    level = jnp.exp(jax.random.uniform(keys[1], lead, jnp.float32, -2.3, 2.3))
    depth = jax.random.uniform(keys[2], lead, jnp.float32, 0.0, 1.5)
    cycles = jax.random.randint(keys[3], lead, 1, 5).astype(jnp.float32)
    phase = jax.random.uniform(keys[4], lead, jnp.float32, -math.pi, math.pi)
    position = jnp.arange(FREQ, dtype=jnp.float32) / FREQ
    envelope = jnp.exp(depth * jnp.cos(2.0 * math.pi * cycles * position + phase))
    return (rough * level * envelope).astype(jnp.float32)


def draw_slot_order(key, part):
    keys = jax.random.split(jax.random.fold_in(key, 23), CHANNELS // CH_DEV)
    orders = jax.vmap(lambda single: jax.random.permutation(single, CH_DEV))(keys)
    return orders.reshape(-1).astype(jnp.int32)


def set_ends(array, key, smallest, top_value):
    spot = [jax.random.randint(jax.random.fold_in(key, axis), (), 0, length) for axis, length in enumerate(array.shape)]
    main_axis = array.shape.index(max(array.shape))
    neighbour = spot[:main_axis] + [(spot[main_axis] + 1) % array.shape[main_axis]] + spot[main_axis + 1:]
    return array.at[tuple(spot)].set(smallest).at[tuple(neighbour)].set(top_value)


def setup_inputs(seed: int = 0) -> dict:
    arg_keys = jax.random.split(jax.random.key(seed), 4)
    raw_spectra = draw_raw_spectra(jax.random.fold_in(arg_keys[3], 71), 0)
    seg_valid = set_ends((jax.random.randint(arg_keys[1], (CHANNELS, SEG), 0, 4) < 3).astype(jnp.int32), jax.random.fold_in(arg_keys[1], 1), 0, 1)
    slot_order = draw_slot_order(jax.random.fold_in(arg_keys[3], 71), 0)
    return dict(raw_spectra=raw_spectra, seg_valid=seg_valid, slot_order=slot_order)


def whiten(raw, valid):
    amplitude = jnp.sqrt(raw[:, :, 0, :] * raw[:, :, 0, :] + raw[:, :, 1, :] * raw[:, :, 1, :])
    bins = jnp.arange(FREQ, dtype=jnp.int32)
    band = (jnp.abs(bins[:, None] - bins[None, :]) <= HALF_BAND).astype(jnp.float32)
    counts = lax.optimization_barrier(jnp.sum(band, axis=0))
    smooth = jnp.einsum('csf,fg->csg', amplitude, band, precision=lax.Precision.HIGHEST) / counts
    scaled = raw / (smooth + 1e-06)[:, :, None, :] * valid.astype(jnp.float32)[:, :, None, None]
    return scaled.astype(jnp.bfloat16)

def lag_table():
    bins = jnp.arange(FREQ, dtype=jnp.int32)
    shifts = jnp.arange(LAGS, dtype=jnp.int32)
    product = bins[:, None] * shifts[None, :] % (2 * FREQ)
    angle = product.astype(jnp.float32) * jnp.float32(math.pi / FREQ)
    return (jnp.cos(angle) * jnp.float32(1.0 / math.sqrt(SEG * FREQ))).astype(jnp.bfloat16)

def reference(raw_spectra, seg_valid, slot_order):
    white = whiten(raw_spectra, seg_valid)
    base = jnp.arange(CHANNELS, dtype=jnp.int32) // CH_DEV * CH_DEV
    chosen = (base + slot_order).astype(jnp.int32)
    column_channel = chosen.reshape(N_ROW, N_COL, CH_DEV).transpose(1, 0, 2).reshape(-1)
    columns = white[column_channel].astype(jnp.float32)
    table = lag_table().astype(jnp.float32)

    def tile(rows):
        cross = jnp.einsum('asxf,bsxf->fab', rows.astype(jnp.float32), columns).astype(jnp.bfloat16)
        return jnp.einsum('fab,ft->abt', cross.astype(jnp.float32), table).astype(jnp.bfloat16)
    blocks = white.reshape(N_ROW, ROW_BLOCK, SEG, 2, FREQ)
    result = lax.map(tile, blocks)
    return result.reshape(CHANNELS, CHANNELS, LAGS)
```

```python
import functools
import math

import jax
import jax.numpy as jnp
from jax import lax
from jax.experimental import pallas as pl
from jax.experimental.pallas import tpu as pltpu
from jax.sharding import Mesh, PartitionSpec as P

CH = 5
SEG = 64
FREQ = 512
LAGS = 512
HALF_BAND = 64
K = 2 * SEG
HALF = FREQ // 2
N_X, N_YL, N_Z, N_YH, N_C = 4, 2, 8, 2, 2
SIZES = {"x": N_X, "yl": N_YL, "z": N_Z, "yh": N_YH, "c": N_C}
COLS = 40
BOTH = 2 * COLS
FB = 128
VMEM = 56 * 1024 * 1024


def lag_table():
    bins = jnp.arange(FREQ, dtype=jnp.int32)
    shifts = jnp.arange(LAGS, dtype=jnp.int32)
    product = bins[:, None] * shifts[None, :] % (2 * FREQ)
    angle = product.astype(jnp.float32) * jnp.float32(math.pi / FREQ)
    return (jnp.cos(angle) * jnp.float32(1.0 / math.sqrt(SEG * FREQ))).astype(jnp.bfloat16)


def shift(x, axis, step):
    n = SIZES[axis]
    return lax.ppermute(x, axis, [(i, (i + step) % n) for i in range(n)])


def params():
    return pltpu.CompilerParams(vmem_limit_bytes=VMEM)


def whiten_kernel(scal, raw, valid, mine, other):
    c = scal[0]
    rows = lax.broadcasted_iota(jnp.int32, (FREQ, FREQ), 0)
    cols = lax.broadcasted_iota(jnp.int32, (FREQ, FREQ), 1)
    band = (jnp.abs(rows - cols) <= HALF_BAND).astype(jnp.bfloat16)
    bins = lax.broadcasted_iota(jnp.int32, (1, FREQ), 1)
    count = jnp.minimum(bins + HALF_BAND, FREQ - 1) - jnp.maximum(bins - HALF_BAND, 0) + 1
    count = count.astype(jnp.float32)

    def part(j, x):
        tiles = [raw[pl.ds(j * SEG * 8 + 2 * b + x, SEG, stride=8), :] for b in range(4)]
        return jnp.concatenate(tiles, axis=1)

    for j in range(CH):
        re, im = part(j, 0), part(j, 1)
        amp = jnp.sqrt(re * re + im * im)
        hi = amp.astype(jnp.bfloat16)
        left = amp - hi.astype(jnp.float32)
        mid = left.astype(jnp.bfloat16)
        low = (left - mid.astype(jnp.float32)).astype(jnp.bfloat16)
        total = jnp.dot(hi, band, preferred_element_type=jnp.float32)
        total += jnp.dot(mid, band, preferred_element_type=jnp.float32)
        total += jnp.dot(low, band, preferred_element_type=jnp.float32)
        smooth = total / count + 1e-06
        keep = valid[j * SEG : (j + 1) * SEG, :].astype(jnp.float32)
        white = jnp.concatenate([re / smooth * keep, im / smooth * keep], axis=0)
        for b in range(4):
            tile = white[:, b * 128 : (b + 1) * 128].T.astype(jnp.bfloat16)
            at = (pl.ds((b % 2) * 128, 128), pl.ds(j * K, K))

            @pl.when(c == b // 2)
            def _():
                mine[(0,) + at] = tile

            @pl.when(c != b // 2)
            def _():
                other[(0,) + at] = tile

    for k in range(CH):
        src = pl.ds(pl.multiple_of(scal[1 + k] * K, K), K)
        mine[1, :, pl.ds(k * K, K)] = mine[0, :, src]
        other[1, :, pl.ds(k * K, K)] = other[0, :, src]


def whiten(raw, valid, order, c):
    view = raw.reshape(CH, SEG, 2, 4, 128).transpose(0, 1, 3, 2, 4).reshape(CH * SEG * 8, 128)
    scal = jnp.concatenate([c.reshape(1), order]).astype(jnp.int32)
    msg = jax.ShapeDtypeStruct((2, HALF, CH * K), jnp.bfloat16)
    return pl.pallas_call(
        whiten_kernel,
        out_shape=(msg, msg),
        in_specs=[
            pl.BlockSpec(memory_space=pltpu.SMEM),
            pl.BlockSpec(memory_space=pltpu.VMEM),
            pl.BlockSpec(memory_space=pltpu.VMEM),
        ],
        out_specs=(pl.BlockSpec(memory_space=pltpu.VMEM),) * 2,
        compiler_params=params(),
        cost_estimate=pl.CostEstimate(flops=10**9, bytes_accessed=3 * 10**6, transcendentals=0),
        name="whiten",
    )(scal, view, valid.reshape(CH * SEG, 1))


def columns_kernel(scal, *refs):
    pieces, out, flat = refs[:8], refs[8], refs[9]
    block = out.shape[0]
    for p in range(8):
        r = scal[p]
        for q in range(2):
            for k in range(CH):
                at = pl.multiple_of((q * COLS + r * CH + k) * block, block)
                flat[pl.ds(at, block), :] = pieces[p][q, :, k * K : (k + 1) * K].astype(jnp.float32)

    def body(i, carry):
        for u in range(8):
            f = i * 8 + u
            out[f] = flat[pl.ds(f, BOTH, stride=block), :].astype(jnp.bfloat16)
        return carry

    lax.fori_loop(0, block // 8, body, 0)


def columns(scal, pieces):
    block = 64
    piece = pl.BlockSpec((2, block, CH * K), lambda i, s: (0, i, 0))
    return pl.pallas_call(
        columns_kernel,
        out_shape=jax.ShapeDtypeStruct((HALF, BOTH, K), jnp.bfloat16),
        grid_spec=pltpu.PrefetchScalarGridSpec(
            num_scalar_prefetch=1,
            grid=(HALF // block,),
            in_specs=[piece] * 8,
            out_specs=pl.BlockSpec((block, BOTH, K), lambda i, s: (i, 0, 0)),
            scratch_shapes=[pltpu.VMEM((BOTH * block, K), jnp.float32)],
        ),
        compiler_params=params(),
        cost_estimate=pl.CostEstimate(flops=10**8, bytes_accessed=20 * 10**6, transcendentals=0),
        name="columns",
    )(scal, *pieces)


def cross_kernel(n, scal, *refs):
    pieces, cols, keep, send, flat, acc = refs[: 2 * n], refs[2 * n], *refs[2 * n + 1 :]
    rows = 20 * n
    c, yh = scal[0], scal[1]
    for p in range(2 * n):
        g, h = p // 2, p % 2
        for q in range(2):
            base = g * 20 + (yh ^ h) * 10 + (c ^ q) * 5
            for k in range(CH):
                at = pl.multiple_of((base + k) * FB, FB)
                flat[pl.ds(at, FB), :] = pieces[p][q, :, k * K : (k + 1) * K].astype(jnp.float32)

    def body(i, carry):
        for u in range(8):
            f = i * 8 + u
            first = flat[pl.ds(f, rows, stride=FB), :].astype(jnp.bfloat16)
            pair = lax.dot_general(
                first, cols[f], (((1,), (1,)), ((), ())), preferred_element_type=jnp.float32
            )
            acc[pl.ds(f, rows, stride=FB), 0:BOTH] = pair
        return carry

    lax.fori_loop(0, FB // 8, body, 0)
    for a in range(rows):
        tile = acc[a * FB : (a + 1) * FB, :].T
        keep[a] = tile[0:COLS].astype(jnp.bfloat16)
        send[a] = tile[COLS:BOTH].astype(jnp.bfloat16)


def cross(scal, pieces, cols):
    n = len(pieces) // 2
    rows = 20 * n
    piece = pl.BlockSpec((2, FB, CH * K), lambda i, s: (0, i, 0))
    part = pl.BlockSpec((rows, COLS, FB), lambda i, s: (0, 0, i))
    shape = jax.ShapeDtypeStruct((rows, COLS, HALF), jnp.bfloat16)
    return pl.pallas_call(
        functools.partial(cross_kernel, n),
        out_shape=(shape, shape),
        grid_spec=pltpu.PrefetchScalarGridSpec(
            num_scalar_prefetch=1,
            grid=(HALF // FB,),
            in_specs=[piece] * (2 * n) + [pl.BlockSpec((FB, BOTH, K), lambda i, s: (i, 0, 0))],
            out_specs=(part, part),
            scratch_shapes=[pltpu.VMEM((rows * FB, K), jnp.float32)] * 2,
        ),
        compiler_params=params(),
        cost_estimate=pl.CostEstimate(flops=10**10, bytes_accessed=10**7, transcendentals=0),
        name="cross",
    )(scal, *pieces, cols)


def lags_kernel(scal, keep, recv, near, far, *rest):
    out = rest[-1]
    total = jnp.dot(keep[...], near[0], preferred_element_type=jnp.float32)
    total += jnp.dot(recv[...], far[0], preferred_element_type=jnp.float32)
    out[...] = total.astype(jnp.bfloat16)


def lags(scal, keep, recv, table, prior):
    n = keep.shape[0] // 20
    rows = 20 * COLS
    half = pl.BlockSpec((rows, HALF), lambda i, s: (i, 0))
    extra = [] if prior is None else [prior]
    return pl.pallas_call(
        lags_kernel,
        out_shape=jax.ShapeDtypeStruct((N_Z * rows, LAGS), jnp.bfloat16),
        grid_spec=pltpu.PrefetchScalarGridSpec(
            num_scalar_prefetch=1,
            grid=(n,),
            in_specs=[
                half,
                half,
                pl.BlockSpec((1, HALF, LAGS), lambda i, s: (s[0], 0, 0)),
                pl.BlockSpec((1, HALF, LAGS), lambda i, s: (1 - s[0], 0, 0)),
            ]
            + [pl.BlockSpec(memory_space=pl.ANY)] * len(extra),
            out_specs=pl.BlockSpec((rows, LAGS), lambda i, s: (s[1 + i], 0)),
        ),
        input_output_aliases={5: 0} if extra else {},
        compiler_params=params(),
        cost_estimate=pl.CostEstimate(flops=2 * 10**9, bytes_accessed=3 * 10**6, transcendentals=0),
        name="lags",
    )(scal, keep.reshape(n * rows, HALF), recv.reshape(n * rows, HALF), table, table, *extra)


def shards(raw_spectra, seg_valid, slot_order):
    x, yl, z, yh, c = (lax.axis_index(a).astype(jnp.int32) for a in ("x", "yl", "z", "yh", "c"))
    mine, other = whiten(raw_spectra, seg_valid, slot_order, c)
    got = shift(other, "c", 1)
    row = jnp.stack([mine[0], got[0]])
    col = jnp.stack([mine[1], got[1]])
    table = lag_table().reshape(2, HALF, LAGS)

    R, C = {(0, 0): row}, {(0, 0): col}
    R[1, 0], R[-1, 0] = shift(row, "z", 1), shift(row, "z", -1)
    C[1, 0], C[-1, 0] = shift(col, "x", 1), shift(col, "x", -1)
    R[0, 1], C[0, 1] = shift(row, "yh", 1), shift(col, "yl", 1)
    R[2, 0], R[-2, 0] = shift(R[1, 0], "z", 1), shift(R[-1, 0], "z", -1)
    C[1, 1], C[-1, 1] = shift(C[0, 1], "x", 1), shift(C[0, 1], "x", -1)
    C[2, 0], C[2, 1] = shift(C[1, 0], "x", 1), shift(C[-1, 1], "x", -1)
    R[3, 0], R[-3, 0] = shift(R[2, 0], "z", 1), shift(R[-2, 0], "z", -1)
    R[4, 0] = shift(R[3, 0], "z", 1)
    for d in (1, -1, 2, -2, 3, -3, 4):
        step = 1 if d > 0 else -1
        R[d, 1] = shift(R[d, 0], "yh", 1) if d in (3, 4) else shift(R[d - step, 1], "z", step)

    order = [(dx, dy) for dx in (0, 1, -1, 2) for dy in (0, 1)]
    rows_of = jnp.stack([((x - dx) % N_X) * N_YL + (yl ^ dy) for dx, dy in order])
    cols = columns(rows_of, [C[o] for o in order])

    here = jnp.stack([c, yh])
    out = None
    for group in ((0,), (1, -1), (2, -2), (3, -3), (4,)):
        pieces = [R[d, h] for d in group for h in (0, 1)]
        keep, send = cross(here, pieces, cols)
        recv = shift(send, "c", 1)
        place = jnp.stack([c] + [(z - d) % N_Z for d in group])
        out = lags(place, keep, recv, table, out)
    return out.reshape(N_Z * 20, COLS, LAGS)


def solution(mesh):
    fine = Mesh(mesh.devices.reshape(N_X, N_YL, N_Z, N_YH, N_C), ("x", "yl", "z", "yh", "c"))
    every = ("x", "yl", "z", "yh", "c")
    return jax.shard_map(
        shards,
        mesh=fine,
        in_specs=(P(every, None, None, None), P(every, None), P(every)),
        out_specs=P(("x", "yl"), ("z", "yh", "c"), None),
        check_vma=False,
    )
```

```python
import functools
import math

import jax
import jax.numpy as jnp
import numpy as np
from jax import lax
from jax.experimental import pallas as pl
from jax.experimental.pallas import tpu as pltpu
from jax.sharding import Mesh, PartitionSpec as P

CH = 5
SEG = 64
FREQ = 512
LAGS = 512
HALF_BAND = 64
K = 2 * SEG
HALF = FREQ // 2
N_X, N_YL, N_Z, N_YH, N_C = 4, 2, 8, 2, 2
SIZES = {"x": N_X, "yl": N_YL, "z": N_Z, "yh": N_YH, "c": N_C}
COLS = 40
BOTH = 2 * COLS
FB = 128
VMEM = 60 * 1024 * 1024


def lag_table():
    product = np.arange(FREQ)[:, None] * np.arange(LAGS)[None, :] % (2 * FREQ)
    wave = np.cos(product * (math.pi / FREQ)) / math.sqrt(SEG * FREQ)
    return jnp.asarray(wave.astype(np.float32)).astype(jnp.bfloat16).reshape(2, HALF, LAGS)


def shift(x, axis, step):
    n = SIZES[axis]
    return lax.ppermute(x, axis, [(i, (i + step) % n) for i in range(n)])


def params():
    return pltpu.CompilerParams(vmem_limit_bytes=VMEM)


def whiten_kernel(scal, raw, valid, mine, other):
    c = scal[4]
    rows = lax.broadcasted_iota(jnp.int32, (FREQ, FREQ), 0)
    cols = lax.broadcasted_iota(jnp.int32, (FREQ, FREQ), 1)
    band = (jnp.abs(rows - cols) <= HALF_BAND).astype(jnp.bfloat16)
    bins = lax.broadcasted_iota(jnp.int32, (1, FREQ), 1)
    count = jnp.minimum(bins + HALF_BAND, FREQ - 1) - jnp.maximum(bins - HALF_BAND, 0) + 1
    count = count.astype(jnp.float32)

    def part(x):
        tiles = [raw[pl.ds(2 * b + x, CH * SEG, stride=8), :] for b in range(4)]
        return jnp.concatenate(tiles, axis=1)

    re, im = part(0), part(1)
    amp = jnp.sqrt(re * re + im * im)
    hi = amp.astype(jnp.bfloat16)
    left = amp - hi.astype(jnp.float32)
    mid = left.astype(jnp.bfloat16)
    low = (left - mid.astype(jnp.float32)).astype(jnp.bfloat16)
    parts = jnp.concatenate([hi, mid, low], axis=0)
    sums = jnp.dot(parts, band, preferred_element_type=jnp.float32)
    n = CH * SEG
    smooth = (sums[:n] + sums[n : 2 * n] + sums[2 * n :]) / count + 1e-06
    scale = 1.0 / smooth
    re, im = re * scale, im * scale
    for j in range(CH):
        keep = valid[j : j + 1, :].astype(jnp.float32)
        keep = jnp.concatenate([keep, keep], axis=1)
        for b in range(4):
            at = (slice(j * SEG, (j + 1) * SEG), slice(b * 128, (b + 1) * 128))
            tile = jnp.concatenate([re[at], im[at]], axis=0).T
            tile = (tile * keep).astype(jnp.bfloat16)
            to = (0, pl.ds((b % 2) * 128, 128), pl.ds(j * K, K))

            @pl.when(c == b // 2)
            def _():
                mine[to] = tile

            @pl.when(c != b // 2)
            def _():
                other[to] = tile

    for k in range(CH):
        src = pl.ds(pl.multiple_of(scal[5 + k] * K, K), K)
        mine[1, :, pl.ds(k * K, K)] = mine[0, :, src]
        other[1, :, pl.ds(k * K, K)] = other[0, :, src]


def whiten(scal, raw, valid):
    view = raw.reshape(CH, SEG, 2, 4, 128).transpose(0, 1, 3, 2, 4).reshape(CH * SEG * 8, 128)
    msg = jax.ShapeDtypeStruct((2, HALF, CH * K), jnp.bfloat16)
    return pl.pallas_call(
        whiten_kernel,
        out_shape=(msg, msg),
        in_specs=[
            pl.BlockSpec(memory_space=pltpu.SMEM),
            pl.BlockSpec(memory_space=pltpu.VMEM),
            pl.BlockSpec(memory_space=pltpu.VMEM),
        ],
        out_specs=(pl.BlockSpec(memory_space=pltpu.VMEM),) * 2,
        compiler_params=params(),
        cost_estimate=pl.CostEstimate(flops=10**9, bytes_accessed=3 * 10**6, transcendentals=0),
        name="whiten",
    )(scal, view, valid)


ORDER = [(dx, dy) for dx in (0, 1, -1, 2) for dy in (0, 1)]
UNROLL = 16


def cross_kernel(n, scal, *refs):
    rows = 20 * n
    pieces, cols = refs[: 2 * n], refs[2 * n : 2 * n + 8]
    keep, send, flat, side, acc = refs[2 * n + 8 :]
    x, yl, yh, c = scal[0], scal[1], scal[3], scal[4]

    def spread(piece, q, into, base):
        for k in range(CH):
            at = pl.multiple_of((base + k) * FB, FB)
            into[pl.ds(at, FB), :] = piece[q, :, k * K : (k + 1) * K].astype(jnp.float32)

    for p in range(8):
        dx, dy = ORDER[p]
        r = lax.rem(x - dx + N_X, N_X) * N_YL + (yl ^ dy)
        for q in range(2):
            spread(cols[p], q, side, q * COLS + r * CH)
    for p in range(2 * n):
        for q in range(2):
            spread(pieces[p], q, flat, (p // 2) * 20 + (yh ^ (p % 2)) * 10 + (c ^ q) * 5)

    def body(i, carry):
        at = [i * UNROLL + u for u in range(UNROLL)]
        pairs = []
        for f in at:
            first = flat[pl.ds(f, rows, stride=FB), :].astype(jnp.bfloat16)
            second = side[pl.ds(f, BOTH, stride=FB), :].astype(jnp.bfloat16)
            pairs.append(
                lax.dot_general(
                    first, second, (((1,), (1,)), ((), ())), preferred_element_type=jnp.float32
                )
            )
        for f, pair in zip(at, pairs):
            acc[pl.ds(f, rows, stride=FB), 0:BOTH] = pair
        return carry

    lax.fori_loop(0, FB // UNROLL, body, 0)
    for a in range(rows):
        tile = acc[a * FB : (a + 1) * FB, :].T
        keep[a] = tile[0:COLS].astype(jnp.bfloat16)
        send[a] = tile[COLS:BOTH].astype(jnp.bfloat16)


def cross(scal, pieces, cols):
    n = len(pieces) // 2
    rows = 20 * n
    piece = pl.BlockSpec((2, FB, CH * K), lambda i, s: (0, i, 0))
    part = pl.BlockSpec((rows, COLS, FB), lambda i, s: (0, 0, i))
    shape = jax.ShapeDtypeStruct((rows, COLS, HALF), jnp.bfloat16)
    return pl.pallas_call(
        functools.partial(cross_kernel, n),
        out_shape=(shape, shape),
        grid_spec=pltpu.PrefetchScalarGridSpec(
            num_scalar_prefetch=1,
            grid=(HALF // FB,),
            in_specs=[piece] * (2 * n + 8),
            out_specs=(part, part),
            scratch_shapes=[
                pltpu.VMEM((rows * FB, K), jnp.float32),
                pltpu.VMEM((BOTH * FB, K), jnp.float32),
                pltpu.VMEM((rows * FB, K), jnp.float32),
            ],
        ),
        compiler_params=params(),
        cost_estimate=pl.CostEstimate(flops=10**10, bytes_accessed=10**7, transcendentals=0),
        name="cross",
    )(scal, *pieces, *cols)


def lags_kernel(scal, keep, recv, near, far, *rest):
    out = rest[-1]
    total = jnp.dot(keep[...], near[0], preferred_element_type=jnp.float32)
    total += jnp.dot(recv[...], far[0], preferred_element_type=jnp.float32)
    out[...] = total.astype(jnp.bfloat16)


def lags(scal, group, keep, recv, table, prior):
    n = len(group)
    rows = 20 * COLS
    half = pl.BlockSpec((rows, HALF), lambda i, s: (i, 0))
    extra = [] if prior is None else [prior]

    def place(i, s):
        back = sum(jnp.where(i == g, d, 0) for g, d in enumerate(group))
        return lax.rem(s[2] - back + N_Z, N_Z), 0

    return pl.pallas_call(
        lags_kernel,
        out_shape=jax.ShapeDtypeStruct((N_Z * rows, LAGS), jnp.bfloat16),
        grid_spec=pltpu.PrefetchScalarGridSpec(
            num_scalar_prefetch=1,
            grid=(n,),
            in_specs=[
                half,
                half,
                pl.BlockSpec((1, HALF, LAGS), lambda i, s: (s[4], 0, 0)),
                pl.BlockSpec((1, HALF, LAGS), lambda i, s: (1 - s[4], 0, 0)),
            ]
            + [pl.BlockSpec(memory_space=pl.ANY)] * len(extra),
            out_specs=pl.BlockSpec((rows, LAGS), place),
        ),
        input_output_aliases={5: 0} if extra else {},
        compiler_params=params(),
        cost_estimate=pl.CostEstimate(flops=2 * 10**9, bytes_accessed=3 * 10**6, transcendentals=0),
        name="lags",
    )(scal, keep.reshape(n * rows, HALF), recv.reshape(n * rows, HALF), table, table, *extra)


GROUPS = ((0, 1, -1, 2, -2), (3, -3, 4))


def shards(raw_spectra, seg_valid, slot_order):
    where = [lax.axis_index(a).astype(jnp.int32) for a in ("x", "yl", "z", "yh", "c")]
    scal = jnp.concatenate([jnp.stack(where), slot_order])
    mine, other = whiten(scal, raw_spectra, seg_valid)
    got = shift(other, "c", 1)
    row = jnp.stack([mine[0], got[0]])
    col = jnp.stack([mine[1], got[1]])
    table = lag_table()

    R, C = {(0, 0): row}, {(0, 0): col}
    R[1, 0], R[-1, 0] = shift(row, "z", 1), shift(row, "z", -1)
    C[1, 0], C[-1, 0] = shift(col, "x", 1), shift(col, "x", -1)
    R[0, 1] = shift(row, "yh", 1)
    late, R[0, 1] = lax.optimization_barrier((col, R[0, 1]))
    C[0, 1] = shift(late, "yl", 1)
    R[2, 0], R[-2, 0] = shift(R[1, 0], "z", 1), shift(R[-1, 0], "z", -1)
    C[1, 1], C[-1, 1] = shift(C[0, 1], "x", 1), shift(C[0, 1], "x", -1)
    C[2, 0], C[2, 1] = shift(C[1, 0], "x", 1), shift(C[-1, 1], "x", -1)
    R[3, 0], R[-3, 0] = shift(R[2, 0], "z", 1), shift(R[-2, 0], "z", -1)
    R[4, 0] = shift(R[3, 0], "z", 1)
    for d in (1, -1, 2, -2, 3, -3, 4):
        step = 1 if d > 0 else -1
        R[d, 1] = shift(R[d, 0], "yh", 1) if d in (3, 4) else shift(R[d - step, 1], "z", step)

    cols = [C[o] for o in ORDER]
    out = None
    for g, group in enumerate(GROUPS):
        pieces = [R[d, h] for d in group for h in (0, 1)]
        if g == 0:
            pieces, _, _ = lax.optimization_barrier((pieces, R[4, 0], R[-2, 1]))
        keep, send = cross(scal, pieces, cols)
        recv = shift(send, "c", 1)
        out = lags(scal, group, keep, recv, table, out)
    return out.reshape(N_Z * 20, COLS, LAGS)


def solution(mesh):
    fine = Mesh(mesh.devices.reshape(N_X, N_YL, N_Z, N_YH, N_C), ("x", "yl", "z", "yh", "c"))
    every = ("x", "yl", "z", "yh", "c")
    return jax.shard_map(
        shards,
        mesh=fine,
        in_specs=(P(every, None, None, None), P(every, None), P(every)),
        out_specs=P(("x", "yl"), ("z", "yh", "c"), None),
        check_vma=False,
    )
```

```python
import functools
import math

import jax
import jax.numpy as jnp
import numpy as np
from jax import lax
from jax.experimental import pallas as pl
from jax.experimental.pallas import tpu as pltpu
from jax.sharding import Mesh, PartitionSpec as P

CH = 5
SEG = 64
FREQ = 512
LAGS = 512
HALF_BAND = 64
K = 2 * SEG
HALF = FREQ // 2
N_X, N_YL, N_Z, N_YH, N_C = 4, 2, 8, 2, 2
SIZES = {"x": N_X, "yl": N_YL, "z": N_Z, "yh": N_YH, "c": N_C}
COLS = 40
BOTH = 2 * COLS
FB = 128
VMEM = 60 * 1024 * 1024


def lag_table():
    product = np.arange(FREQ)[:, None] * np.arange(LAGS)[None, :] % (2 * FREQ)
    wave = np.cos(product * (math.pi / FREQ)) / math.sqrt(SEG * FREQ)
    return jnp.asarray(wave.astype(np.float32)).astype(jnp.bfloat16).reshape(2, HALF, LAGS)


def shift(x, axis, step):
    n = SIZES[axis]
    return lax.ppermute(x, axis, [(i, (i + step) % n) for i in range(n)])


def params():
    return pltpu.CompilerParams(vmem_limit_bytes=VMEM)


def whiten_kernel(scal, raw, valid, mine, other):
    c = scal[4]
    rows = lax.broadcasted_iota(jnp.int32, (FREQ, FREQ), 0)
    cols = lax.broadcasted_iota(jnp.int32, (FREQ, FREQ), 1)
    band = (jnp.abs(rows - cols) <= HALF_BAND).astype(jnp.bfloat16)
    bins = lax.broadcasted_iota(jnp.int32, (1, FREQ), 1)
    count = jnp.minimum(bins + HALF_BAND, FREQ - 1) - jnp.maximum(bins - HALF_BAND, 0) + 1
    count = count.astype(jnp.float32)

    def part(x):
        tiles = [raw[pl.ds(2 * b + x, CH * SEG, stride=8), :] for b in range(4)]
        return jnp.concatenate(tiles, axis=1)

    re, im = part(0), part(1)
    amp = jnp.sqrt(re * re + im * im)
    hi = amp.astype(jnp.bfloat16)
    left = amp - hi.astype(jnp.float32)
    mid = left.astype(jnp.bfloat16)
    low = (left - mid.astype(jnp.float32)).astype(jnp.bfloat16)
    parts = jnp.concatenate([hi, mid, low], axis=0)
    sums = jnp.dot(parts, band, preferred_element_type=jnp.float32)
    n = CH * SEG
    smooth = (sums[:n] + sums[n : 2 * n] + sums[2 * n :]) / count + 1e-06
    scale = 1.0 / smooth
    re, im = re * scale, im * scale
    for j in range(CH):
        keep = valid[j : j + 1, :].astype(jnp.float32)
        keep = jnp.concatenate([keep, keep], axis=1)
        for b in range(4):
            at = (slice(j * SEG, (j + 1) * SEG), slice(b * 128, (b + 1) * 128))
            tile = jnp.concatenate([re[at], im[at]], axis=0).T
            tile = (tile * keep).astype(jnp.bfloat16)
            to = (0, pl.ds((b % 2) * 128, 128), pl.ds(j * K, K))

            @pl.when(c == b // 2)
            def _():
                mine[to] = tile

            @pl.when(c != b // 2)
            def _():
                other[to] = tile

    for k in range(CH):
        src = pl.ds(pl.multiple_of(scal[5 + k] * K, K), K)
        mine[1, :, pl.ds(k * K, K)] = mine[0, :, src]
        other[1, :, pl.ds(k * K, K)] = other[0, :, src]


def whiten(scal, raw, valid):
    view = raw.reshape(CH, SEG, 2, 4, 128).transpose(0, 1, 3, 2, 4).reshape(CH * SEG * 8, 128)
    msg = jax.ShapeDtypeStruct((2, HALF, CH * K), jnp.bfloat16)
    return pl.pallas_call(
        whiten_kernel,
        out_shape=(msg, msg),
        in_specs=[
            pl.BlockSpec(memory_space=pltpu.SMEM),
            pl.BlockSpec(memory_space=pltpu.VMEM),
            pl.BlockSpec(memory_space=pltpu.VMEM),
        ],
        out_specs=(pl.BlockSpec(memory_space=pltpu.VMEM),) * 2,
        compiler_params=params(),
        cost_estimate=pl.CostEstimate(flops=10**9, bytes_accessed=3 * 10**6, transcendentals=0),
        name="whiten",
    )(scal, view, valid)


UNROLL = 16
PITCH = FB + 8
STEPS = (0, 1, -1, 2)


def cross_kernel(n, scal, *refs):
    rows = 10 * n
    pieces, cols = refs[:n], refs[n : n + 8]
    keep, send, flat, side, acc = refs[n + 8 :]
    x, yl, c = scal[0], scal[1], scal[4]

    def spread(piece, into, base):
        for k in range(CH):
            at = pl.multiple_of((base + k) * PITCH, 8)
            into[pl.ds(at, FB), :] = piece[:, k * K : (k + 1) * K].astype(jnp.float32)

    for p in range(4):
        for h in range(2):
            r = lax.rem(x - STEPS[p] + N_X, N_X) * N_YL + (yl ^ h)
            for q in range(2):
                spread(cols[2 * p + h].at[q], side, q * COLS + r * CH)
    for p in range(n):
        for q in range(2):
            spread(pieces[p].at[q], flat, p * 10 + (c ^ q) * 5)

    def body(i, carry):
        at = [i * UNROLL + u for u in range(UNROLL)]
        pairs = []
        for f in at:
            first = flat[pl.ds(f, rows, stride=PITCH), :].astype(jnp.bfloat16)
            second = side[pl.ds(f, BOTH, stride=PITCH), :].astype(jnp.bfloat16)
            pairs.append(
                lax.dot_general(
                    first, second, (((1,), (1,)), ((), ())), preferred_element_type=jnp.float32
                )
            )
        for f, pair in zip(at, pairs):
            acc[pl.ds(f, rows, stride=PITCH), 0:BOTH] = pair
        return carry

    lax.fori_loop(0, FB // UNROLL, body, 0)
    for a in range(rows):
        tile = acc[a * PITCH : a * PITCH + FB, :].T
        keep[a] = tile[0:COLS].astype(jnp.bfloat16)
        send[a] = tile[COLS:BOTH].astype(jnp.bfloat16)


def cross(scal, pieces, cols):
    n = len(pieces)
    rows = 10 * n
    piece = pl.BlockSpec((2, FB, CH * K), lambda i, s: (0, i, 0))
    part = pl.BlockSpec((rows, COLS, FB), lambda i, s: (0, 0, i))
    shape = jax.ShapeDtypeStruct((rows, COLS, HALF), jnp.bfloat16)
    return pl.pallas_call(
        functools.partial(cross_kernel, n),
        out_shape=(shape, shape),
        grid_spec=pltpu.PrefetchScalarGridSpec(
            num_scalar_prefetch=1,
            grid=(HALF // FB,),
            in_specs=[piece] * (n + 8),
            out_specs=(part, part),
            scratch_shapes=[
                pltpu.VMEM((rows * PITCH, K), jnp.float32),
                pltpu.VMEM((BOTH * PITCH, K), jnp.float32),
                pltpu.VMEM((rows * PITCH, K), jnp.float32),
            ],
        ),
        compiler_params=params(),
        cost_estimate=pl.CostEstimate(flops=10**10, bytes_accessed=10**7, transcendentals=0),
        name="cross",
    )(scal, *pieces, *cols)


def lags_kernel(scal, keep, recv, near, far, *rest):
    both = jnp.concatenate([keep[...], recv[...]], axis=1)
    table = jnp.concatenate([near[0], far[0]], axis=0)
    total = jnp.dot(both, table, preferred_element_type=jnp.float32)
    rest[-1][...] = total.astype(jnp.bfloat16)


def lags(scal, group, keep, recv, table, prior):
    n = len(group)
    rows = 10 * COLS
    half = pl.BlockSpec((rows, HALF), lambda i, s: (i, 0))
    extra = [] if prior is None else [prior]

    def place(i, s):
        back = sum(jnp.where(i == g, d, 0) for g, (d, _) in enumerate(group))
        side = sum(jnp.where(i == g, h, 0) for g, (_, h) in enumerate(group))
        return lax.rem(s[2] - back + N_Z, N_Z) * N_YH + (s[3] ^ side), 0

    return pl.pallas_call(
        lags_kernel,
        out_shape=jax.ShapeDtypeStruct((N_Z * N_YH * rows, LAGS), jnp.bfloat16),
        grid_spec=pltpu.PrefetchScalarGridSpec(
            num_scalar_prefetch=1,
            grid=(n,),
            in_specs=[
                half,
                half,
                pl.BlockSpec((1, HALF, LAGS), lambda i, s: (s[4], 0, 0)),
                pl.BlockSpec((1, HALF, LAGS), lambda i, s: (1 - s[4], 0, 0)),
            ]
            + [pl.BlockSpec(memory_space=pl.ANY)] * len(extra),
            out_specs=pl.BlockSpec((rows, LAGS), place),
        ),
        input_output_aliases={5: 0} if extra else {},
        compiler_params=params(),
        cost_estimate=pl.CostEstimate(flops=2 * 10**9, bytes_accessed=3 * 10**6, transcendentals=0),
        name="lags",
    )(scal, keep.reshape(n * rows, HALF), recv.reshape(n * rows, HALF), table, table, *extra)


OWN = tuple((d, 0) for d in (0, 1, -1, 2, -2, 3, -3))
GROUPS = (
    OWN + ((1, 1), (-1, 1)),
    ((0, 1), (-2, 1), (4, 0), (2, 1), (-3, 1)),
    ((3, 1), (4, 1)),
)


def after(value, *earlier):
    return lax.optimization_barrier((value, earlier))[0]


def shards(raw_spectra, seg_valid, slot_order):
    where = [lax.axis_index(a).astype(jnp.int32) for a in ("x", "yl", "z", "yh", "c")]
    scal = jnp.concatenate([jnp.stack(where), slot_order])
    mine, other = whiten(scal, raw_spectra, seg_valid)
    got = shift(other, "c", 1)
    row = jnp.stack([mine[0], got[0]])
    col = jnp.stack([mine[1], got[1]])
    table = lag_table()

    R, C = {(0, 0): row}, {(0, 0): col}
    R[1, 0], R[-1, 0] = shift(row, "z", 1), shift(row, "z", -1)
    C[0, 1] = shift(col, "yl", 1)
    C[1, 0], C[-1, 0] = shift(col, "x", 1), shift(col, "x", -1)

    R[2, 0] = shift(R[1, 0], "z", 1)
    R[-2, 0] = shift(after(R[-1, 0], R[1, 0]), "z", -1)
    both = shift(after(jnp.stack([R[1, 0], R[-1, 0]]), C[0, 1]), "yh", 1)
    R[1, 1], R[-1, 1] = both[0], both[1]
    C[1, 1] = shift(after(C[0, 1], R[-1, 0], C[1, 0]), "x", 1)
    C[-1, 1] = shift(after(C[0, 1], C[1, 0], C[-1, 0]), "x", -1)

    R[3, 0] = shift(after(R[2, 0], C[-1, 0]), "z", 1)
    R[-3, 0] = shift(after(R[-2, 0], R[2, 0]), "z", -1)
    C[2, 0] = shift(after(C[1, 0], C[1, 1], R[-2, 0]), "x", 1)
    C[2, 1] = shift(after(C[-1, 1], C[1, 1]), "x", -1)
    R[0, 1] = shift(after(row, both, C[-1, 1]), "yh", 1)

    both = shift(after(jnp.stack([R[3, 0], R[1, 1]]), C[-1, 1]), "z", 1)
    R[4, 0], R[2, 1] = both[0], both[1]
    R[-2, 1] = shift(after(R[-1, 1], R[-3, 0], R[3, 0]), "z", -1)
    R[-3, 1] = shift(R[-2, 1], "z", -1)
    R[3, 1] = shift(R[2, 1], "z", 1)
    R[4, 1] = shift(R[-3, 1], "z", -1)

    cols = [C[dx, dy] for dx in STEPS for dy in (0, 1)]
    gates = ((R[3, 0], R[-3, 0]), (R[4, 0], R[-3, 1]), ())
    out = None
    for group, gate in zip(GROUPS, gates):
        pieces = after([R[p] for p in group], *gate)
        keep, send = cross(scal, pieces, cols)
        out = lags(scal, group, keep, shift(send, "c", 1), table, out)
    return out.reshape(N_Z * 20, COLS, LAGS)


def solution(mesh):
    fine = Mesh(mesh.devices.reshape(N_X, N_YL, N_Z, N_YH, N_C), ("x", "yl", "z", "yh", "c"))
    every = ("x", "yl", "z", "yh", "c")
    return jax.shard_map(
        shards,
        mesh=fine,
        in_specs=(P(every, None, None, None), P(every, None), P(every)),
        out_specs=P(("x", "yl"), ("z", "yh", "c"), None),
        check_vma=False,
    )
```

```python
import functools
import math

import jax
import jax.numpy as jnp
import numpy as np
from jax import lax
from jax.experimental import pallas as pl
from jax.experimental.pallas import tpu as pltpu
from jax.sharding import Mesh, PartitionSpec as P

CH = 5
SEG = 64
FREQ = 512
LAGS = 512
HALF_BAND = 64
K = 2 * SEG
HALF = FREQ // 2
N_X, N_YL, N_Z, N_YH, N_C = 4, 2, 8, 2, 2
SIZES = {"x": N_X, "yl": N_YL, "z": N_Z, "yh": N_YH, "c": N_C}
COLS = 40
BOTH = 2 * COLS
FB = 128
VMEM = 24 * 1024 * 1024


def lag_table():
    product = np.arange(FREQ)[:, None] * np.arange(LAGS)[None, :] % (2 * FREQ)
    wave = np.cos(product * (math.pi / FREQ)) / math.sqrt(SEG * FREQ)
    return jnp.asarray(wave.astype(np.float32)).astype(jnp.bfloat16).reshape(2, HALF, LAGS)


def shift(x, axis, step):
    n = SIZES[axis]
    return lax.ppermute(x, axis, [(i, (i + step) % n) for i in range(n)])


def params():
    return pltpu.CompilerParams(vmem_limit_bytes=VMEM)


def whiten_kernel(scal, raw, valid, mine, other):
    c = scal[4]
    rows = lax.broadcasted_iota(jnp.int32, (FREQ, FREQ), 0)
    cols = lax.broadcasted_iota(jnp.int32, (FREQ, FREQ), 1)
    band = (jnp.abs(rows - cols) <= HALF_BAND).astype(jnp.bfloat16)
    bins = lax.broadcasted_iota(jnp.int32, (1, FREQ), 1)
    count = jnp.minimum(bins + HALF_BAND, FREQ - 1) - jnp.maximum(bins - HALF_BAND, 0) + 1
    count = count.astype(jnp.float32)

    def part(x):
        tiles = [raw[pl.ds(2 * b + x, CH * SEG, stride=8), :] for b in range(4)]
        return jnp.concatenate(tiles, axis=1)

    re, im = part(0), part(1)
    amp = jnp.sqrt(re * re + im * im)
    hi = amp.astype(jnp.bfloat16)
    left = amp - hi.astype(jnp.float32)
    mid = left.astype(jnp.bfloat16)
    low = (left - mid.astype(jnp.float32)).astype(jnp.bfloat16)
    parts = jnp.concatenate([hi, mid, low], axis=0)
    sums = jnp.dot(parts, band, preferred_element_type=jnp.float32)
    n = CH * SEG
    smooth = (sums[:n] + sums[n : 2 * n] + sums[2 * n :]) / count + 1e-06
    scale = 1.0 / smooth
    re, im = re * scale, im * scale
    for j in range(CH):
        keep = valid[j : j + 1, :].astype(jnp.float32)
        keep = jnp.concatenate([keep, keep], axis=1)
        for b in range(4):
            at = (slice(j * SEG, (j + 1) * SEG), slice(b * 128, (b + 1) * 128))
            tile = jnp.concatenate([re[at], im[at]], axis=0).T
            tile = (tile * keep).astype(jnp.bfloat16)
            to = (0, pl.ds((b % 2) * 128, 128), pl.ds(j * K, K))

            @pl.when(c == b // 2)
            def _():
                mine[to] = tile

            @pl.when(c != b // 2)
            def _():
                other[to] = tile

    for k in range(CH):
        src = pl.ds(pl.multiple_of(scal[5 + k] * K, K), K)
        mine[1, :, pl.ds(k * K, K)] = mine[0, :, src]
        other[1, :, pl.ds(k * K, K)] = other[0, :, src]


def whiten(scal, raw, valid):
    view = raw.reshape(CH, SEG, 2, 4, 128).transpose(0, 1, 3, 2, 4).reshape(CH * SEG * 8, 128)
    msg = jax.ShapeDtypeStruct((2, HALF, CH * K), jnp.bfloat16)
    return pl.pallas_call(
        whiten_kernel,
        out_shape=(msg, msg),
        in_specs=[
            pl.BlockSpec(memory_space=pltpu.SMEM),
            pl.BlockSpec(memory_space=pltpu.VMEM),
            pl.BlockSpec(memory_space=pltpu.VMEM),
        ],
        out_specs=(pl.BlockSpec(memory_space=pltpu.VMEM),) * 2,
        compiler_params=params(),
        cost_estimate=pl.CostEstimate(flops=10**9, bytes_accessed=3 * 10**6, transcendentals=0),
        name="whiten",
    )(scal, view, valid)


UNROLL = 16
PITCH = FB + 8
STEPS = (0, 1, -1, 2)
MIB = 1024 * 1024


def cross_kernel(n, lead, scal, *refs):
    rows = 10 * n
    pieces, rest = refs[:n], refs[n:]
    x, yl, c = scal[0], scal[1], scal[4]
    if lead:
        cols, (keep, send, packed, flat, acc, side) = rest[:8], rest[8:]
    else:
        packed, keep, send, flat, acc = rest

    def spread(piece, into, base):
        for k in range(CH):
            at = pl.multiple_of((base + k) * PITCH, 8)
            into[pl.ds(at, FB), :] = piece[:, k * K : (k + 1) * K].astype(jnp.float32)

    if lead:
        for p in range(4):
            for h in range(2):
                r = lax.rem(x - STEPS[p] + N_X, N_X) * N_YL + (yl ^ h)
                for q in range(2):
                    spread(cols[2 * p + h].at[q], side, q * COLS + r * CH)
    for p in range(n):
        for q in range(2):
            spread(pieces[p].at[q], flat, p * 10 + (c ^ q) * 5)

    def body(i, carry):
        at = [i * UNROLL + u for u in range(UNROLL)]
        pairs = []
        for f in at:
            first = flat[pl.ds(f, rows, stride=PITCH), :].astype(jnp.bfloat16)
            if lead:
                second = side[pl.ds(f, BOTH, stride=PITCH), :].astype(jnp.bfloat16)
                packed[f] = second
            else:
                second = packed[f]
            pairs.append(
                lax.dot_general(
                    first, second, (((1,), (1,)), ((), ())), preferred_element_type=jnp.float32
                )
            )
        for f, pair in zip(at, pairs):
            acc[pl.ds(f, rows, stride=PITCH), 0:BOTH] = pair
        return carry

    lax.fori_loop(0, FB // UNROLL, body, 0)
    for a in range(rows):
        tile = acc[a * PITCH : a * PITCH + FB, :].T
        keep[a] = tile[0:COLS].astype(jnp.bfloat16)
        send[a] = tile[COLS:BOTH].astype(jnp.bfloat16)


def cross(scal, pieces, cols, lead):
    n = len(pieces)
    rows = 10 * n
    specs, arrays = [], []
    for piece in pieces:
        if isinstance(piece, tuple):
            piece, at = piece
            specs.append(pl.BlockSpec((None, 2, FB, CH * K), lambda i, s, at=at: (at, 0, i, 0)))
        else:
            specs.append(pl.BlockSpec((2, FB, CH * K), lambda i, s: (0, i, 0)))
        arrays.append(piece)
    part = pl.BlockSpec((rows, COLS, FB), lambda i, s: (0, 0, i))
    shape = jax.ShapeDtypeStruct((rows, COLS, HALF), jnp.bfloat16)
    packed = pl.BlockSpec((FB, BOTH, K), lambda i, s: (i, 0, 0))
    held = jax.ShapeDtypeStruct((HALF, BOTH, K), jnp.bfloat16)
    scratch = [pltpu.VMEM((rows * PITCH, K), jnp.float32)] * 2
    if lead:
        specs += [pl.BlockSpec((2, FB, CH * K), lambda i, s: (0, i, 0))] * len(cols)
        scratch.append(pltpu.VMEM((BOTH * PITCH, K), jnp.float32))
    else:
        specs.append(packed)
    return pl.pallas_call(
        functools.partial(cross_kernel, n, lead),
        out_shape=(shape, shape, held) if lead else (shape, shape),
        grid_spec=pltpu.PrefetchScalarGridSpec(
            num_scalar_prefetch=1,
            grid=(HALF // FB,),
            in_specs=specs,
            out_specs=(part, part, packed) if lead else (part, part),
            scratch_shapes=scratch,
        ),
        compiler_params=pltpu.CompilerParams(vmem_limit_bytes=(26 + 3 * n // 2) * MIB),
        cost_estimate=pl.CostEstimate(flops=10**10, bytes_accessed=10**7, transcendentals=0),
        name="cross",
    )(scal, *arrays, *(cols if lead else [cols]))


def lags_kernel(group, scal, keep, recv, table, *rest):
    out, held, sem = rest[-3:]
    rows = 10 * COLS
    z, yh, c = scal[2], scal[3], scal[4]
    copies = []
    for g, (d, h) in enumerate(group):
        at = slice(g * rows, (g + 1) * rows)
        total = jnp.dot(keep[at, :], table[c], preferred_element_type=jnp.float32)
        total += jnp.dot(recv[at, :], table[1 - c], preferred_element_type=jnp.float32)
        held[at, :] = total.astype(jnp.bfloat16)
        to = (lax.rem(z - d + N_Z, N_Z) * N_YH + (yh ^ h)) * rows
        copy = pltpu.make_async_copy(
            held.at[at, :], out.at[pl.ds(pl.multiple_of(to, rows), rows), :], sem.at[g]
        )
        copy.start()
        copies.append(copy)
    for copy in copies:
        copy.wait()


def lags(scal, group, keep, recv, table, prior):
    n = len(group)
    rows = 10 * COLS
    extra = [] if prior is None else [prior]
    vmem = pl.BlockSpec(memory_space=pltpu.VMEM)
    return pl.pallas_call(
        functools.partial(lags_kernel, group),
        out_shape=jax.ShapeDtypeStruct((N_Z * N_YH * rows, LAGS), jnp.bfloat16),
        in_specs=[pl.BlockSpec(memory_space=pltpu.SMEM)]
        + [vmem] * 3
        + [pl.BlockSpec(memory_space=pl.ANY)] * len(extra),
        out_specs=pl.BlockSpec(memory_space=pl.ANY),
        scratch_shapes=[pltpu.VMEM((n * rows, LAGS), jnp.bfloat16), pltpu.SemaphoreType.DMA((n,))],
        input_output_aliases={4: 0} if extra else {},
        compiler_params=pltpu.CompilerParams(vmem_limit_bytes=16 * MIB),
        cost_estimate=pl.CostEstimate(flops=2 * 10**9, bytes_accessed=3 * 10**6, transcendentals=0),
        name="lags",
    )(scal, keep.reshape(n * rows, HALF), recv.reshape(n * rows, HALF), table, *extra)


OWN = tuple((d, 0) for d in (0, 1, -1, 2, -2, 3, -3))
GROUPS = (
    OWN + ((1, 1), (-1, 1)),
    ((0, 1), (-2, 1), (4, 0), (2, 1), (-3, 1)),
    ((3, 1), (4, 1)),
)


def after(value, *earlier):
    return lax.optimization_barrier((value, earlier))[0]


def gate(pieces, *earlier):
    arrays = [p[0] if isinstance(p, tuple) else p for p in pieces]
    arrays, earlier = lax.optimization_barrier((arrays, earlier))
    held = [(a, p[1]) if isinstance(p, tuple) else a for a, p in zip(arrays, pieces)]
    return held, earlier


def shards(raw_spectra, seg_valid, slot_order):
    where = [lax.axis_index(a).astype(jnp.int32) for a in ("x", "yl", "z", "yh", "c")]
    scal = jnp.concatenate([jnp.stack(where), slot_order])
    mine, other = whiten(scal, raw_spectra, seg_valid)
    got = shift(other, "c", 1)
    row = jnp.stack([mine[0], got[0]])
    col = jnp.stack([mine[1], got[1]])
    table = lag_table()

    R, C = {(0, 0): row}, {(0, 0): col}
    R[1, 0], R[-1, 0] = shift(row, "z", 1), shift(row, "z", -1)
    C[0, 1] = shift(col, "yl", 1)
    C[1, 0], C[-1, 0] = shift(col, "x", 1), shift(col, "x", -1)

    R[2, 0] = shift(R[1, 0], "z", 1)
    R[-2, 0] = shift(after(R[-1, 0], R[1, 0]), "z", -1)
    near = shift(after(jnp.stack([R[1, 0], R[-1, 0]]), C[0, 1]), "yh", 1)
    R[1, 1], R[-1, 1] = (near, 0), (near, 1)
    C[1, 1] = shift(after(C[0, 1], R[-1, 0], C[1, 0]), "x", 1)
    C[-1, 1] = shift(after(C[0, 1], C[1, 0], C[-1, 0]), "x", -1)

    R[3, 0] = shift(after(R[2, 0], C[-1, 0]), "z", 1)
    R[-3, 0] = shift(after(R[-2, 0], R[2, 0]), "z", -1)
    C[2, 0] = shift(after(C[1, 0], C[1, 1], R[-2, 0]), "x", 1)
    C[2, 1] = shift(after(C[-1, 1], C[1, 1]), "x", -1)
    R[0, 1] = shift(after(row, near, C[-1, 1]), "yh", 1)

    far = shift(after(jnp.stack([R[3, 0], near[0]]), C[-1, 1]), "z", 1)
    R[4, 0], R[2, 1] = (far, 0), (far, 1)
    R[-2, 1] = shift(after(near[1], R[-3, 0], R[3, 0]), "z", -1)
    R[-3, 1] = shift(after(R[-2, 1], C[2, 0], C[2, 1]), "z", -1)
    R[3, 1] = shift(far[1], "z", 1)
    R[4, 1] = shift(R[-3, 1], "z", -1)

    cols = [C[dx, dy] for dx in STEPS for dy in (0, 1)]
    own = [R[p] for p in GROUPS[0]]
    keep, send, cols = cross(scal, gate(own, R[3, 0], R[-3, 0])[0], cols, True)
    recv = shift(send, "c", 1)
    own, _ = gate([R[p] for p in GROUPS[1]], far, R[-3, 1])
    keep1, send1 = cross(scal, own, cols, False)
    recv1 = shift(send1, "c", 1)
    out = lags(scal, GROUPS[0], keep, recv, table, None)
    own, (out,) = gate([R[p] for p in GROUPS[2]], out)
    keep2, send2 = cross(scal, own, cols, False)
    recv2 = shift(send2, "c", 1)
    out = lags(scal, GROUPS[1], keep1, recv1, table, out)
    out = lags(scal, GROUPS[2], keep2, recv2, table, out)
    return out.reshape(N_Z * 20, COLS, LAGS)


def solution(mesh):
    fine = Mesh(mesh.devices.reshape(N_X, N_YL, N_Z, N_YH, N_C), ("x", "yl", "z", "yh", "c"))
    every = ("x", "yl", "z", "yh", "c")
    return jax.shard_map(
        shards,
        mesh=fine,
        in_specs=(P(every, None, None, None), P(every, None), P(every)),
        out_specs=P(("x", "yl"), ("z", "yh", "c"), None),
        check_vma=False,
    )
```

```python
import functools
import math

import jax
import jax.numpy as jnp
import numpy as np
from jax import lax
from jax.experimental import pallas as pl
from jax.experimental.pallas import tpu as pltpu
from jax.sharding import Mesh, PartitionSpec as P

CH = 5
SEG = 64
FREQ = 512
LAGS = 512
HALF_BAND = 64
K = 2 * SEG
HALF = FREQ // 2
N_X, N_YL, N_Z, N_YH, N_C = 4, 2, 8, 2, 2
SIZES = {"x": N_X, "yl": N_YL, "z": N_Z, "yh": N_YH, "c": N_C}
COLS = 40
BOTH = 2 * COLS
FB = 128
VMEM = 24 * 1024 * 1024


def lag_table():
    product = np.arange(FREQ)[:, None] * np.arange(LAGS)[None, :] % (2 * FREQ)
    wave = np.cos(product * (math.pi / FREQ)) / math.sqrt(SEG * FREQ)
    return jnp.asarray(wave.astype(np.float32)).astype(jnp.bfloat16).reshape(2, HALF, LAGS)


def shift(x, axis, step):
    n = SIZES[axis]
    return lax.ppermute(x, axis, [(i, (i + step) % n) for i in range(n)])


def params():
    return pltpu.CompilerParams(vmem_limit_bytes=VMEM)


def whiten_kernel(scal, raw, valid, mine, other):
    c = scal[4]
    rows = lax.broadcasted_iota(jnp.int32, (FREQ, FREQ), 0)
    cols = lax.broadcasted_iota(jnp.int32, (FREQ, FREQ), 1)
    band = (jnp.abs(rows - cols) <= HALF_BAND).astype(jnp.bfloat16)
    bins = lax.broadcasted_iota(jnp.int32, (1, FREQ), 1)
    count = jnp.minimum(bins + HALF_BAND, FREQ - 1) - jnp.maximum(bins - HALF_BAND, 0) + 1
    count = count.astype(jnp.float32)

    def part(x):
        tiles = [raw[pl.ds(2 * b + x, CH * SEG, stride=8), :] for b in range(4)]
        return jnp.concatenate(tiles, axis=1)

    re, im = part(0), part(1)
    amp = jnp.sqrt(re * re + im * im)
    hi = amp.astype(jnp.bfloat16)
    left = amp - hi.astype(jnp.float32)
    mid = left.astype(jnp.bfloat16)
    low = (left - mid.astype(jnp.float32)).astype(jnp.bfloat16)
    parts = jnp.concatenate([hi, mid, low], axis=0)
    sums = jnp.dot(parts, band, preferred_element_type=jnp.float32)
    n = CH * SEG
    smooth = (sums[:n] + sums[n : 2 * n] + sums[2 * n :]) / count + 1e-06
    scale = 1.0 / smooth
    re, im = re * scale, im * scale
    for j in range(CH):
        keep = valid[j : j + 1, :].astype(jnp.float32)
        keep = jnp.concatenate([keep, keep], axis=1)
        for b in range(4):
            at = (slice(j * SEG, (j + 1) * SEG), slice(b * 128, (b + 1) * 128))
            tile = jnp.concatenate([re[at], im[at]], axis=0).T
            tile = (tile * keep).astype(jnp.bfloat16)
            to = (0, pl.ds((b % 2) * 128, 128), pl.ds(j * K, K))

            @pl.when(c == b // 2)
            def _():
                mine[to] = tile

            @pl.when(c != b // 2)
            def _():
                other[to] = tile

    for k in range(CH):
        src = pl.ds(pl.multiple_of(scal[5 + k] * K, K), K)
        mine[1, :, pl.ds(k * K, K)] = mine[0, :, src]
        other[1, :, pl.ds(k * K, K)] = other[0, :, src]


def whiten(scal, raw, valid):
    view = raw.reshape(CH, SEG, 2, 4, 128).transpose(0, 1, 3, 2, 4).reshape(CH * SEG * 8, 128)
    msg = jax.ShapeDtypeStruct((2, HALF, CH * K), jnp.bfloat16)
    return pl.pallas_call(
        whiten_kernel,
        out_shape=(msg, msg),
        in_specs=[
            pl.BlockSpec(memory_space=pltpu.SMEM),
            pl.BlockSpec(memory_space=pltpu.VMEM),
            pl.BlockSpec(memory_space=pltpu.VMEM),
        ],
        out_specs=(pl.BlockSpec(memory_space=pltpu.VMEM),) * 2,
        compiler_params=params(),
        cost_estimate=pl.CostEstimate(flops=10**9, bytes_accessed=3 * 10**6, transcendentals=0),
        name="whiten",
    )(scal, view, valid)


UNROLL = 32
PITCH = FB + 8
STEPS = (0, 1, -1, 2)
MIB = 1024 * 1024


def cross_kernel(n, lead, indices, scal, *refs):
    rows = 10 * n
    pieces, rest = refs[:n], refs[n:]
    x, yl, c = scal[0], scal[1], scal[4]
    if lead:
        cols, (keep, send, packed, flat, acc, side) = rest[:8], rest[8:]
    else:
        packed, keep, send, flat, acc = rest

    def spread(piece, q, start, into, base):
        for k in range(CH):
            at = pl.multiple_of((base + k) * PITCH, 8)
            tile = piece[q, pl.ds(start, FB), k * K : (k + 1) * K]
            into[pl.ds(at, FB), :] = tile.astype(jnp.float32)

    def block(b, carry):
        start = pl.multiple_of(b * FB, FB)
        if lead:
            for p in range(4):
                for h in range(2):
                    r = lax.rem(x - STEPS[p] + N_X, N_X) * N_YL + (yl ^ h)
                    for q in range(2):
                        spread(cols[2 * p + h], q, start, side, q * COLS + r * CH)
        for p, index in enumerate(indices):
            piece = pieces[p] if index is None else pieces[p].at[index]
            for q in range(2):
                spread(piece, q, start, flat, p * 10 + (c ^ q) * 5)

        def body(i, carry):
            at = [i * UNROLL + u for u in range(UNROLL)]
            pairs = []
            for f in at:
                first = flat[pl.ds(f, rows, stride=PITCH), :].astype(jnp.bfloat16)
                if lead:
                    second = side[pl.ds(f, BOTH, stride=PITCH), :].astype(jnp.bfloat16)
                    packed[start + f] = second
                else:
                    second = packed[start + f]
                pairs.append(
                    lax.dot_general(
                        first,
                        second,
                        (((1,), (1,)), ((), ())),
                        preferred_element_type=jnp.float32,
                    )
                )
            for f, pair in zip(at, pairs):
                acc[pl.ds(f, rows, stride=PITCH), 0:BOTH] = pair
            return carry

        lax.fori_loop(0, FB // UNROLL, body, 0)
        for a in range(rows):
            tile = acc[a * PITCH : a * PITCH + FB, :].T
            keep[a, :, pl.ds(start, FB)] = tile[0:COLS].astype(jnp.bfloat16)
            send[a, :, pl.ds(start, FB)] = tile[COLS:BOTH].astype(jnp.bfloat16)
        return carry

    lax.fori_loop(0, HALF // FB, block, 0)


def cross(scal, pieces, cols, lead):
    n = len(pieces)
    rows = 10 * n
    arrays = [p[0] if isinstance(p, tuple) else p for p in pieces]
    indices = [p[1] if isinstance(p, tuple) else None for p in pieces]
    arrays += list(cols) if lead else [cols]
    shape = jax.ShapeDtypeStruct((rows, COLS, HALF), jnp.bfloat16)
    held = jax.ShapeDtypeStruct((HALF, BOTH, K), jnp.bfloat16)
    outs = (shape, shape, held) if lead else (shape, shape)
    scratch = [pltpu.VMEM((rows * PITCH, K), jnp.float32)] * 2
    if lead:
        scratch.append(pltpu.VMEM((BOTH * PITCH, K), jnp.float32))
    vmem = pl.BlockSpec(memory_space=pltpu.VMEM)
    return pl.pallas_call(
        functools.partial(cross_kernel, n, lead, indices),
        out_shape=outs,
        in_specs=[pl.BlockSpec(memory_space=pltpu.SMEM)] + [vmem] * len(arrays),
        out_specs=(vmem,) * len(outs),
        scratch_shapes=scratch,
        compiler_params=pltpu.CompilerParams(vmem_limit_bytes=(12 + 3 * n // 2) * MIB),
        cost_estimate=pl.CostEstimate(flops=10**10, bytes_accessed=10**7, transcendentals=0),
        name="cross",
    )(scal, *arrays)


def lags_kernel(group, scal, keep, recv, table, *rest):
    out, held, sem = rest[-3:]
    rows = 10 * COLS
    z, yh, c = scal[2], scal[3], scal[4]
    copies = []
    for g, (d, h) in enumerate(group):
        at = slice(g * rows, (g + 1) * rows)
        total = jnp.dot(keep[at, :], table[c], preferred_element_type=jnp.float32)
        total += jnp.dot(recv[at, :], table[1 - c], preferred_element_type=jnp.float32)
        held[at, :] = total.astype(jnp.bfloat16)
        to = (lax.rem(z - d + N_Z, N_Z) * N_YH + (yh ^ h)) * rows
        copy = pltpu.make_async_copy(
            held.at[at, :], out.at[pl.ds(pl.multiple_of(to, rows), rows), :], sem.at[g]
        )
        copy.start()
        copies.append(copy)
    for copy in copies:
        copy.wait()


def lags(scal, group, keep, recv, table, prior):
    n = len(group)
    rows = 10 * COLS
    extra = [] if prior is None else [prior]
    vmem = pl.BlockSpec(memory_space=pltpu.VMEM)
    return pl.pallas_call(
        functools.partial(lags_kernel, group),
        out_shape=jax.ShapeDtypeStruct((N_Z * N_YH * rows, LAGS), jnp.bfloat16),
        in_specs=[pl.BlockSpec(memory_space=pltpu.SMEM)]
        + [vmem] * 3
        + [pl.BlockSpec(memory_space=pl.ANY)] * len(extra),
        out_specs=pl.BlockSpec(memory_space=pl.ANY),
        scratch_shapes=[pltpu.VMEM((n * rows, LAGS), jnp.bfloat16), pltpu.SemaphoreType.DMA((n,))],
        input_output_aliases={4: 0} if extra else {},
        compiler_params=pltpu.CompilerParams(vmem_limit_bytes=16 * MIB),
        cost_estimate=pl.CostEstimate(flops=2 * 10**9, bytes_accessed=3 * 10**6, transcendentals=0),
        name="lags",
    )(scal, keep.reshape(n * rows, HALF), recv.reshape(n * rows, HALF), table, *extra)


OWN = tuple((d, 0) for d in (0, 1, -1, 2, -2, 3, -3))
GROUPS = (
    OWN + ((1, 1), (-1, 1)),
    ((0, 1), (-2, 1), (4, 0), (2, 1), (-3, 1)),
    ((3, 1), (4, 1)),
)


def after(value, *earlier):
    return lax.optimization_barrier((value, earlier))[0]


def gate(pieces, *earlier):
    arrays = [p[0] if isinstance(p, tuple) else p for p in pieces]
    arrays, earlier = lax.optimization_barrier((arrays, earlier))
    held = [(a, p[1]) if isinstance(p, tuple) else a for a, p in zip(arrays, pieces)]
    return held, earlier


def shards(raw_spectra, seg_valid, slot_order):
    where = [lax.axis_index(a).astype(jnp.int32) for a in ("x", "yl", "z", "yh", "c")]
    scal = jnp.concatenate([jnp.stack(where), slot_order])
    mine, other = whiten(scal, raw_spectra, seg_valid)
    got = shift(other, "c", 1)
    row = jnp.stack([mine[0], got[0]])
    col = jnp.stack([mine[1], got[1]])
    table = lag_table()

    R, C = {(0, 0): row}, {(0, 0): col}
    R[1, 0], R[-1, 0] = shift(row, "z", 1), shift(row, "z", -1)
    C[0, 1] = shift(col, "yl", 1)
    C[1, 0], C[-1, 0] = shift(col, "x", 1), shift(col, "x", -1)

    R[2, 0] = shift(R[1, 0], "z", 1)
    R[-2, 0] = shift(after(R[-1, 0], R[1, 0]), "z", -1)
    near = shift(after(jnp.stack([R[1, 0], R[-1, 0]]), C[0, 1], C[1, 0]), "yh", 1)
    R[1, 1], R[-1, 1] = (near, 0), (near, 1)
    C[1, 1] = shift(after(C[0, 1], R[-1, 0], C[1, 0]), "x", 1)
    C[-1, 1] = shift(after(C[0, 1], C[1, 0], C[-1, 0]), "x", -1)

    R[3, 0] = shift(after(R[2, 0], C[-1, 0]), "z", 1)
    R[-3, 0] = shift(after(R[-2, 0], R[2, 0]), "z", -1)
    C[2, 0] = shift(after(C[1, 0], C[1, 1], R[-2, 0]), "x", 1)
    C[2, 1] = shift(after(C[-1, 1], C[1, 1]), "x", -1)
    R[0, 1] = shift(after(row, near, C[-1, 1]), "yh", 1)

    far = shift(after(jnp.stack([R[3, 0], near[0]]), C[-1, 1]), "z", 1)
    R[4, 0], R[2, 1] = (far, 0), (far, 1)
    R[-2, 1] = shift(after(near[1], R[-3, 0], R[3, 0]), "z", -1)
    R[-3, 1] = shift(after(R[-2, 1], C[2, 0], C[2, 1]), "z", -1)
    R[3, 1] = shift(far[1], "z", 1)
    R[4, 1] = shift(R[-3, 1], "z", -1)

    cols = [C[dx, dy] for dx in STEPS for dy in (0, 1)]
    own = [R[p] for p in GROUPS[0]]
    keep, send, cols = cross(scal, gate(own, R[3, 0], R[-3, 0])[0], cols, True)
    recv = shift(send, "c", 1)
    own, _ = gate([R[p] for p in GROUPS[1]], far, R[-3, 1])
    keep1, send1 = cross(scal, own, cols, False)
    recv1 = shift(send1, "c", 1)
    out = lags(scal, GROUPS[0], keep, recv, table, None)
    own, (out,) = gate([R[p] for p in GROUPS[2]], out)
    keep2, send2 = cross(scal, own, cols, False)
    recv2 = shift(send2, "c", 1)
    out = lags(scal, GROUPS[1], keep1, recv1, table, out)
    out = lags(scal, GROUPS[2], keep2, recv2, table, out)
    return out.reshape(N_Z * 20, COLS, LAGS)


def solution(mesh):
    fine = Mesh(mesh.devices.reshape(N_X, N_YL, N_Z, N_YH, N_C), ("x", "yl", "z", "yh", "c"))
    every = ("x", "yl", "z", "yh", "c")
    return jax.shard_map(
        shards,
        mesh=fine,
        in_specs=(P(every, None, None, None), P(every, None), P(every)),
        out_specs=P(("x", "yl"), ("z", "yh", "c"), None),
        check_vma=False,
    )
```

```python
import functools
import math

import jax
import jax.numpy as jnp
import numpy as np
from jax import lax
from jax.experimental import pallas as pl
from jax.experimental.pallas import tpu as pltpu
from jax.sharding import Mesh, PartitionSpec as P

CH = 5
SEG = 64
FREQ = 512
LAGS = 512
HALF_BAND = 64
K = 2 * SEG
HALF = FREQ // 2
N_X, N_YL, N_Z, N_YH, N_C = 4, 2, 8, 2, 2
SIZES = {"x": N_X, "yl": N_YL, "z": N_Z, "yh": N_YH, "c": N_C}
COLS = 40
BOTH = 2 * COLS
FB = 128
VMEM = 24 * 1024 * 1024


def lag_table():
    product = np.arange(FREQ)[:, None] * np.arange(LAGS)[None, :] % (2 * FREQ)
    wave = np.cos(product * (math.pi / FREQ)) / math.sqrt(SEG * FREQ)
    return jnp.asarray(wave.astype(np.float32)).astype(jnp.bfloat16).reshape(2, HALF, LAGS)


def shift(x, axis, step):
    n = SIZES[axis]
    return lax.ppermute(x, axis, [(i, (i + step) % n) for i in range(n)])


def params():
    return pltpu.CompilerParams(vmem_limit_bytes=VMEM)


def whiten_kernel(scal, raw, valid, mine, other):
    c = scal[4]
    rows = lax.broadcasted_iota(jnp.int32, (FREQ, FREQ), 0)
    cols = lax.broadcasted_iota(jnp.int32, (FREQ, FREQ), 1)
    band = (jnp.abs(rows - cols) <= HALF_BAND).astype(jnp.bfloat16)
    bins = lax.broadcasted_iota(jnp.int32, (1, FREQ), 1)
    count = jnp.minimum(bins + HALF_BAND, FREQ - 1) - jnp.maximum(bins - HALF_BAND, 0) + 1
    count = count.astype(jnp.float32)

    def part(x):
        tiles = [raw[pl.ds(2 * b + x, CH * SEG, stride=8), :] for b in range(4)]
        return jnp.concatenate(tiles, axis=1)

    re, im = part(0), part(1)
    amp = jnp.sqrt(re * re + im * im)
    hi = amp.astype(jnp.bfloat16)
    left = amp - hi.astype(jnp.float32)
    mid = left.astype(jnp.bfloat16)
    low = (left - mid.astype(jnp.float32)).astype(jnp.bfloat16)
    parts = jnp.concatenate([hi, mid, low], axis=0)
    sums = jnp.dot(parts, band, preferred_element_type=jnp.float32)
    n = CH * SEG
    smooth = (sums[:n] + sums[n : 2 * n] + sums[2 * n :]) / count + 1e-06
    scale = 1.0 / smooth
    re, im = re * scale, im * scale
    for j in range(CH):
        keep = valid[j : j + 1, :].astype(jnp.float32)
        keep = jnp.concatenate([keep, keep], axis=1)
        for b in range(4):
            at = (slice(j * SEG, (j + 1) * SEG), slice(b * 128, (b + 1) * 128))
            tile = jnp.concatenate([re[at], im[at]], axis=0).T
            tile = (tile * keep).astype(jnp.bfloat16)
            to = (0, pl.ds((b % 2) * 128, 128), pl.ds(j * K, K))

            @pl.when(c == b // 2)
            def _():
                mine[to] = tile

            @pl.when(c != b // 2)
            def _():
                other[to] = tile

    for k in range(CH):
        src = pl.ds(pl.multiple_of(scal[5 + k] * K, K), K)
        mine[1, :, pl.ds(k * K, K)] = mine[0, :, src]
        other[1, :, pl.ds(k * K, K)] = other[0, :, src]


def whiten(scal, raw, valid):
    view = raw.reshape(CH, SEG, 2, 4, 128).transpose(0, 1, 3, 2, 4).reshape(CH * SEG * 8, 128)
    msg = jax.ShapeDtypeStruct((2, HALF, CH * K), jnp.bfloat16)
    return pl.pallas_call(
        whiten_kernel,
        out_shape=(msg, msg),
        in_specs=[
            pl.BlockSpec(memory_space=pltpu.SMEM),
            pl.BlockSpec(memory_space=pltpu.VMEM),
            pl.BlockSpec(memory_space=pltpu.VMEM),
        ],
        out_specs=(pl.BlockSpec(memory_space=pltpu.VMEM),) * 2,
        compiler_params=params(),
        cost_estimate=pl.CostEstimate(flops=10**9, bytes_accessed=3 * 10**6, transcendentals=0),
        name="whiten",
    )(scal, view, valid)


UNROLL = 32
PITCH = FB + 8
STEPS = (0, 1, -1, 2)
MIB = 1024 * 1024


def cross_kernel(n, lead, indices, scal, *refs):
    rows = 10 * n
    pieces, rest = refs[:n], refs[n:]
    x, yl, c = scal[0], scal[1], scal[4]
    if lead:
        cols, (keep, send, packed, flat, acc, side) = rest[:8], rest[8:]
    else:
        packed, keep, send, flat, acc = rest

    def spread(piece, q, start, into, base):
        for k in range(CH):
            at = pl.multiple_of((base + k) * PITCH, 8)
            tile = piece[q, pl.ds(start, FB), k * K : (k + 1) * K]
            into[pl.ds(at, FB), :] = tile.astype(jnp.float32)

    def block(b, carry):
        start = pl.multiple_of(b * FB, FB)
        if lead:
            for p in range(4):
                for h in range(2):
                    r = lax.rem(x - STEPS[p] + N_X, N_X) * N_YL + (yl ^ h)
                    for q in range(2):
                        spread(cols[2 * p + h], q, start, side, q * COLS + r * CH)
        for p, index in enumerate(indices):
            piece = pieces[p] if index is None else pieces[p].at[index]
            for q in range(2):
                spread(piece, q, start, flat, p * 10 + (c ^ q) * 5)

        def body(i, carry):
            at = [i * UNROLL + u for u in range(UNROLL)]
            pairs = []
            for f in at:
                first = flat[pl.ds(f, rows, stride=PITCH), :].astype(jnp.bfloat16)
                if lead:
                    second = side[pl.ds(f, BOTH, stride=PITCH), :].astype(jnp.bfloat16)
                    packed[start + f] = second
                else:
                    second = packed[start + f]
                pairs.append(
                    lax.dot_general(
                        first,
                        second,
                        (((1,), (1,)), ((), ())),
                        preferred_element_type=jnp.float32,
                    )
                )
            for f, pair in zip(at, pairs):
                acc[pl.ds(f, rows, stride=PITCH), 0:BOTH] = pair
            return carry

        lax.fori_loop(0, FB // UNROLL, body, 0)
        for a in range(rows):
            tile = acc[a * PITCH : a * PITCH + FB, :].T
            keep[a, :, pl.ds(start, FB)] = tile[0:COLS].astype(jnp.bfloat16)
            send[a, :, pl.ds(start, FB)] = tile[COLS:BOTH].astype(jnp.bfloat16)
        return carry

    lax.fori_loop(0, HALF // FB, block, 0)


def cross(scal, pieces, cols, lead):
    n = len(pieces)
    rows = 10 * n
    arrays = [p[0] if isinstance(p, tuple) else p for p in pieces]
    indices = [p[1] if isinstance(p, tuple) else None for p in pieces]
    arrays += list(cols) if lead else [cols]
    shape = jax.ShapeDtypeStruct((rows, COLS, HALF), jnp.bfloat16)
    held = jax.ShapeDtypeStruct((HALF, BOTH, K), jnp.bfloat16)
    outs = (shape, shape, held) if lead else (shape, shape)
    scratch = [pltpu.VMEM((rows * PITCH, K), jnp.float32)] * 2
    if lead:
        scratch.append(pltpu.VMEM((BOTH * PITCH, K), jnp.float32))
    vmem = pl.BlockSpec(memory_space=pltpu.VMEM)
    return pl.pallas_call(
        functools.partial(cross_kernel, n, lead, indices),
        out_shape=outs,
        in_specs=[pl.BlockSpec(memory_space=pltpu.SMEM)] + [vmem] * len(arrays),
        out_specs=(vmem,) * len(outs),
        scratch_shapes=scratch,
        compiler_params=pltpu.CompilerParams(vmem_limit_bytes=(12 + 3 * n // 2) * MIB),
        cost_estimate=pl.CostEstimate(flops=10**10, bytes_accessed=10**7, transcendentals=0),
        name="cross",
    )(scal, *arrays)


def lags_kernel(group, scal, keep, recv, table, *rest):
    out, held, sem = rest[-3:]
    rows = 10 * COLS
    z, yh, c = scal[2], scal[3], scal[4]
    copies = []
    for g, (d, h) in enumerate(group):
        at = slice(g * rows, (g + 1) * rows)
        total = jnp.dot(keep[at, :], table[c], preferred_element_type=jnp.float32)
        total += jnp.dot(recv[at, :], table[1 - c], preferred_element_type=jnp.float32)
        held[at, :] = total.astype(jnp.bfloat16)
        to = (lax.rem(z - d + N_Z, N_Z) * N_YH + (yh ^ h)) * rows
        copy = pltpu.make_async_copy(
            held.at[at, :], out.at[pl.ds(pl.multiple_of(to, rows), rows), :], sem.at[g]
        )
        copy.start()
        copies.append(copy)
    for copy in copies:
        copy.wait()


def lags(scal, group, keep, recv, table, prior):
    n = len(group)
    rows = 10 * COLS
    extra = [] if prior is None else [prior]
    vmem = pl.BlockSpec(memory_space=pltpu.VMEM)
    return pl.pallas_call(
        functools.partial(lags_kernel, group),
        out_shape=jax.ShapeDtypeStruct((N_Z * N_YH * rows, LAGS), jnp.bfloat16),
        in_specs=[pl.BlockSpec(memory_space=pltpu.SMEM)]
        + [vmem] * 3
        + [pl.BlockSpec(memory_space=pl.ANY)] * len(extra),
        out_specs=pl.BlockSpec(memory_space=pl.ANY),
        scratch_shapes=[pltpu.VMEM((n * rows, LAGS), jnp.bfloat16), pltpu.SemaphoreType.DMA((n,))],
        input_output_aliases={4: 0} if extra else {},
        compiler_params=pltpu.CompilerParams(vmem_limit_bytes=16 * MIB),
        cost_estimate=pl.CostEstimate(flops=2 * 10**9, bytes_accessed=3 * 10**6, transcendentals=0),
        name="lags",
    )(scal, keep.reshape(n * rows, HALF), recv.reshape(n * rows, HALF), table, *extra)


OWN = tuple((d, 0) for d in (0, 1, -1, 2, -2, 3, -3))
GROUPS = (
    OWN + ((1, 1), (-1, 1)),
    ((-2, 1), (4, 0), (2, 1), (-3, 1)),
    ((0, 1), (3, 1), (4, 1)),
)


def after(value, *earlier):
    return lax.optimization_barrier((value, earlier))[0]


def gate(pieces, *earlier):
    arrays = [p[0] if isinstance(p, tuple) else p for p in pieces]
    arrays, earlier = lax.optimization_barrier((arrays, earlier))
    held = [(a, p[1]) if isinstance(p, tuple) else a for a, p in zip(arrays, pieces)]
    return held, earlier


def shards(raw_spectra, seg_valid, slot_order):
    where = [lax.axis_index(a).astype(jnp.int32) for a in ("x", "yl", "z", "yh", "c")]
    scal = jnp.concatenate([jnp.stack(where), slot_order])
    mine, other = whiten(scal, raw_spectra, seg_valid)
    got = shift(other, "c", 1)
    row = jnp.stack([mine[0], got[0]])
    col = jnp.stack([mine[1], got[1]])
    table = lag_table()

    R, C = {(0, 0): row}, {(0, 0): col}
    R[1, 0], R[-1, 0] = shift(row, "z", 1), shift(row, "z", -1)
    C[0, 1] = shift(col, "yl", 1)
    C[1, 0], C[-1, 0] = shift(col, "x", 1), shift(col, "x", -1)

    R[2, 0] = shift(R[1, 0], "z", 1)
    R[-2, 0] = shift(after(R[-1, 0], R[1, 0]), "z", -1)
    R[-1, 1] = shift(after(R[-1, 0], C[0, 1], C[1, 0]), "yh", 1)
    R[1, 1] = shift(after(R[1, 0], R[-1, 1]), "yh", 1)
    C[1, 1] = shift(after(C[0, 1], R[-1, 0], C[1, 0]), "x", 1)
    C[-1, 1] = shift(after(C[0, 1], C[1, 0], C[-1, 0]), "x", -1)

    R[3, 0] = shift(after(R[2, 0], C[-1, 0]), "z", 1)
    R[-3, 0] = shift(after(R[-2, 0], R[2, 0]), "z", -1)
    C[2, 0] = shift(after(C[1, 0], C[1, 1], R[-2, 0]), "x", 1)
    C[2, 1] = shift(after(C[-1, 1], C[1, 1]), "x", -1)

    far = shift(after(jnp.stack([R[3, 0], R[1, 1]]), C[-1, 1]), "z", 1)
    R[4, 0], R[2, 1] = (far, 0), (far, 1)
    R[-2, 1] = shift(after(R[-1, 1], R[-3, 0], R[3, 0]), "z", -1)
    R[-3, 1] = shift(after(R[-2, 1], C[2, 0], C[2, 1]), "z", -1)
    R[3, 1] = shift(far[1], "z", 1)
    R[4, 1] = shift(R[-3, 1], "z", -1)

    cols = [C[dx, dy] for dx in STEPS for dy in (0, 1)]
    own = [R[p] for p in GROUPS[0]]
    keep, send, cols = cross(scal, gate(own, R[3, 0], R[-3, 0])[0], cols, True)
    R[0, 1] = shift(after(row, keep), "yh", 1)
    recv = shift(send, "c", 1)
    own, _ = gate([R[p] for p in GROUPS[1]], far, R[-3, 1])
    keep1, send1 = cross(scal, own, cols, False)
    recv1 = shift(send1, "c", 1)
    out = lags(scal, GROUPS[0], keep, recv, table, None)
    own, (out,) = gate([R[p] for p in GROUPS[2]], out)
    keep2, send2 = cross(scal, own, cols, False)
    recv2 = shift(send2, "c", 1)
    out = lags(scal, GROUPS[1], keep1, recv1, table, out)
    out = lags(scal, GROUPS[2], keep2, recv2, table, out)
    return out.reshape(N_Z * 20, COLS, LAGS)


def solution(mesh):
    fine = Mesh(mesh.devices.reshape(N_X, N_YL, N_Z, N_YH, N_C), ("x", "yl", "z", "yh", "c"))
    every = ("x", "yl", "z", "yh", "c")
    return jax.shard_map(
        shards,
        mesh=fine,
        in_specs=(P(every, None, None, None), P(every, None), P(every)),
        out_specs=P(("x", "yl"), ("z", "yh", "c"), None),
        check_vma=False,
    )
```

```python
import functools
import math

import jax
import jax.numpy as jnp
import numpy as np
from jax import lax
from jax.experimental import pallas as pl
from jax.experimental.pallas import tpu as pltpu
from jax.sharding import Mesh, PartitionSpec as P

CH = 5
SEG = 64
FREQ = 512
LAGS = 512
HALF_BAND = 64
K = 2 * SEG
HALF = FREQ // 2
N_X, N_YL, N_Z, N_YH, N_C = 4, 2, 8, 2, 2
SIZES = {"x": N_X, "yl": N_YL, "z": N_Z, "yh": N_YH, "c": N_C}
COLS = 40
BOTH = 2 * COLS
FB = 128
VMEM = 24 * 1024 * 1024


def lag_table():
    product = np.arange(FREQ)[:, None] * np.arange(LAGS)[None, :] % (2 * FREQ)
    wave = np.cos(product * (math.pi / FREQ)) / math.sqrt(SEG * FREQ)
    return jnp.asarray(wave.astype(np.float32)).astype(jnp.bfloat16).reshape(2, HALF, LAGS)


def shift(x, axis, step):
    n = SIZES[axis]
    return lax.ppermute(x, axis, [(i, (i + step) % n) for i in range(n)])


def params():
    return pltpu.CompilerParams(vmem_limit_bytes=VMEM)


def whiten_kernel(scal, raw, valid, mine, other):
    c = scal[4]
    rows = lax.broadcasted_iota(jnp.int32, (FREQ, FREQ), 0)
    cols = lax.broadcasted_iota(jnp.int32, (FREQ, FREQ), 1)
    band = (jnp.abs(rows - cols) <= HALF_BAND).astype(jnp.bfloat16)
    bins = lax.broadcasted_iota(jnp.int32, (1, FREQ), 1)
    count = jnp.minimum(bins + HALF_BAND, FREQ - 1) - jnp.maximum(bins - HALF_BAND, 0) + 1
    count = count.astype(jnp.float32)

    def part(x):
        tiles = [raw[pl.ds(2 * b + x, CH * SEG, stride=8), :] for b in range(4)]
        return jnp.concatenate(tiles, axis=1)

    re, im = part(0), part(1)
    amp = jnp.sqrt(re * re + im * im)
    hi = amp.astype(jnp.bfloat16)
    left = amp - hi.astype(jnp.float32)
    mid = left.astype(jnp.bfloat16)
    low = (left - mid.astype(jnp.float32)).astype(jnp.bfloat16)
    parts = jnp.concatenate([hi, mid, low], axis=0)
    sums = jnp.dot(parts, band, preferred_element_type=jnp.float32)
    n = CH * SEG
    smooth = (sums[:n] + sums[n : 2 * n] + sums[2 * n :]) / count + 1e-06
    scale = 1.0 / smooth
    re, im = re * scale, im * scale
    for j in range(CH):
        keep = valid[j : j + 1, :].astype(jnp.float32)
        keep = jnp.concatenate([keep, keep], axis=1)
        for b in range(4):
            at = (slice(j * SEG, (j + 1) * SEG), slice(b * 128, (b + 1) * 128))
            tile = jnp.concatenate([re[at], im[at]], axis=0).T
            tile = (tile * keep).astype(jnp.bfloat16)
            to = (0, pl.ds((b % 2) * 128, 128), pl.ds(j * K, K))

            @pl.when(c == b // 2)
            def _():
                mine[to] = tile

            @pl.when(c != b // 2)
            def _():
                other[to] = tile

    for k in range(CH):
        src = pl.ds(pl.multiple_of(scal[5 + k] * K, K), K)
        mine[1, :, pl.ds(k * K, K)] = mine[0, :, src]
        other[1, :, pl.ds(k * K, K)] = other[0, :, src]


def whiten(scal, raw, valid):
    view = raw.reshape(CH, SEG, 2, 4, 128).transpose(0, 1, 3, 2, 4).reshape(CH * SEG * 8, 128)
    msg = jax.ShapeDtypeStruct((2, HALF, CH * K), jnp.bfloat16)
    return pl.pallas_call(
        whiten_kernel,
        out_shape=(msg, msg),
        in_specs=[
            pl.BlockSpec(memory_space=pltpu.SMEM),
            pl.BlockSpec(memory_space=pltpu.VMEM),
            pl.BlockSpec(memory_space=pltpu.VMEM),
        ],
        out_specs=(pl.BlockSpec(memory_space=pltpu.VMEM),) * 2,
        compiler_params=params(),
        cost_estimate=pl.CostEstimate(flops=10**9, bytes_accessed=3 * 10**6, transcendentals=0),
        name="whiten",
    )(scal, view, valid)


UNROLL = 32
PITCH = FB + 8
STEPS = (0, 1, -1, 2)
MIB = 1024 * 1024


def cross_kernel(n, lead, indices, scal, *refs):
    rows = 10 * n
    pieces, rest = refs[:n], refs[n:]
    x, yl, c = scal[0], scal[1], scal[4]
    if lead:
        cols, (keep, send, packed, flat, acc, side) = rest[:8], rest[8:]
    else:
        packed, keep, send, flat, acc = rest

    def spread(piece, q, start, into, base):
        for k in range(CH):
            at = pl.multiple_of((base + k) * PITCH, 8)
            tile = piece[q, pl.ds(start, FB), k * K : (k + 1) * K]
            into[pl.ds(at, FB), :] = tile.astype(jnp.float32)

    def block(b, carry):
        start = pl.multiple_of(b * FB, FB)
        if lead:
            for p in range(4):
                for h in range(2):
                    r = lax.rem(x - STEPS[p] + N_X, N_X) * N_YL + (yl ^ h)
                    for q in range(2):
                        spread(cols[2 * p + h], q, start, side, q * COLS + r * CH)
        for p, index in enumerate(indices):
            piece = pieces[p] if index is None else pieces[p].at[index]
            for q in range(2):
                spread(piece, q, start, flat, p * 10 + (c ^ q) * 5)

        def body(i, carry):
            at = [i * UNROLL + u for u in range(UNROLL)]
            pairs = []
            for f in at:
                first = flat[pl.ds(f, rows, stride=PITCH), :].astype(jnp.bfloat16)
                if lead:
                    second = side[pl.ds(f, BOTH, stride=PITCH), :].astype(jnp.bfloat16)
                    packed[start + f] = second
                else:
                    second = packed[start + f]
                pairs.append(
                    lax.dot_general(
                        first,
                        second,
                        (((1,), (1,)), ((), ())),
                        preferred_element_type=jnp.float32,
                    )
                )
            for f, pair in zip(at, pairs):
                acc[pl.ds(f, rows, stride=PITCH), 0:BOTH] = pair
            return carry

        lax.fori_loop(0, FB // UNROLL, body, 0)
        for a in range(rows):
            tile = acc[a * PITCH : a * PITCH + FB, :].T
            keep[a, :, pl.ds(start, FB)] = tile[0:COLS].astype(jnp.bfloat16)
            send[a, :, pl.ds(start, FB)] = tile[COLS:BOTH].astype(jnp.bfloat16)
        return carry

    lax.fori_loop(0, HALF // FB, block, 0)


def cross(scal, pieces, cols, lead):
    n = len(pieces)
    rows = 10 * n
    arrays = [p[0] if isinstance(p, tuple) else p for p in pieces]
    indices = [p[1] if isinstance(p, tuple) else None for p in pieces]
    arrays += list(cols) if lead else [cols]
    shape = jax.ShapeDtypeStruct((rows, COLS, HALF), jnp.bfloat16)
    held = jax.ShapeDtypeStruct((HALF, BOTH, K), jnp.bfloat16)
    outs = (shape, shape, held) if lead else (shape, shape)
    scratch = [pltpu.VMEM((rows * PITCH, K), jnp.float32)] * 2
    if lead:
        scratch.append(pltpu.VMEM((BOTH * PITCH, K), jnp.float32))
    vmem = pl.BlockSpec(memory_space=pltpu.VMEM)
    return pl.pallas_call(
        functools.partial(cross_kernel, n, lead, indices),
        out_shape=outs,
        in_specs=[pl.BlockSpec(memory_space=pltpu.SMEM)] + [vmem] * len(arrays),
        out_specs=(vmem,) * len(outs),
        scratch_shapes=scratch,
        compiler_params=pltpu.CompilerParams(vmem_limit_bytes=(12 + 3 * n // 2) * MIB),
        cost_estimate=pl.CostEstimate(flops=10**10, bytes_accessed=10**7, transcendentals=0),
        name="cross",
    )(scal, *arrays)


def lags_kernel(group, scal, keep, recv, table, *rest):
    out, held, sem = rest[-3:]
    rows = 10 * COLS
    z, yh, c = scal[2], scal[3], scal[4]
    copies = []
    for g, (d, h) in enumerate(group):
        at = slice(g * rows, (g + 1) * rows)
        total = jnp.dot(keep[at, :], table[c], preferred_element_type=jnp.float32)
        total += jnp.dot(recv[at, :], table[1 - c], preferred_element_type=jnp.float32)
        held[at, :] = total.astype(jnp.bfloat16)
        to = (lax.rem(z - d + N_Z, N_Z) * N_YH + (yh ^ h)) * rows
        copy = pltpu.make_async_copy(
            held.at[at, :], out.at[pl.ds(pl.multiple_of(to, rows), rows), :], sem.at[g]
        )
        copy.start()
        copies.append(copy)
    for copy in copies:
        copy.wait()


def lags(scal, group, keep, recv, table, prior):
    n = len(group)
    rows = 10 * COLS
    extra = [] if prior is None else [prior]
    vmem = pl.BlockSpec(memory_space=pltpu.VMEM)
    return pl.pallas_call(
        functools.partial(lags_kernel, group),
        out_shape=jax.ShapeDtypeStruct((N_Z * N_YH * rows, LAGS), jnp.bfloat16),
        in_specs=[pl.BlockSpec(memory_space=pltpu.SMEM)]
        + [vmem] * 3
        + [pl.BlockSpec(memory_space=pl.ANY)] * len(extra),
        out_specs=pl.BlockSpec(memory_space=pl.ANY),
        scratch_shapes=[pltpu.VMEM((n * rows, LAGS), jnp.bfloat16), pltpu.SemaphoreType.DMA((n,))],
        input_output_aliases={4: 0} if extra else {},
        compiler_params=pltpu.CompilerParams(vmem_limit_bytes=16 * MIB),
        cost_estimate=pl.CostEstimate(flops=2 * 10**9, bytes_accessed=3 * 10**6, transcendentals=0),
        name="lags",
    )(scal, keep.reshape(n * rows, HALF), recv.reshape(n * rows, HALF), table, *extra)


OWN = tuple((d, 0) for d in (0, 1, -1, 2, -2, 3, -3))
GROUPS = (
    OWN + ((1, 1), (-1, 1)),
    ((-2, 1), (4, 0), (2, 1), (-3, 1)),
    ((0, 1), (3, 1), (4, 1)),
)


def after(value, *earlier):
    return lax.optimization_barrier((value, earlier))[0]


def gate(pieces, *earlier):
    arrays = [p[0] if isinstance(p, tuple) else p for p in pieces]
    arrays, earlier = lax.optimization_barrier((arrays, earlier))
    held = [(a, p[1]) if isinstance(p, tuple) else a for a, p in zip(arrays, pieces)]
    return held, earlier


def shards(raw_spectra, seg_valid, slot_order):
    where = [lax.axis_index(a).astype(jnp.int32) for a in ("x", "yl", "z", "yh", "c")]
    scal = jnp.concatenate([jnp.stack(where), slot_order])
    mine, other = whiten(scal, raw_spectra, seg_valid)
    got = shift(other, "c", 1)
    row = jnp.stack([mine[0], got[0]])
    col = jnp.stack([mine[1], got[1]])
    table = lag_table()

    R, C = {(0, 0): row}, {(0, 0): col}
    R[1, 0], R[-1, 0] = shift(row, "z", 1), shift(row, "z", -1)
    C[0, 1] = shift(col, "yl", 1)
    C[1, 0], C[-1, 0] = shift(col, "x", 1), shift(col, "x", -1)

    R[2, 0] = shift(R[1, 0], "z", 1)
    R[-2, 0] = shift(after(R[-1, 0], R[1, 0]), "z", -1)
    R[-1, 1] = shift(after(R[-1, 0], C[0, 1], C[1, 0]), "yh", 1)
    R[1, 1] = shift(after(R[1, 0], R[-1, 1]), "yh", 1)
    C[1, 1] = shift(after(C[0, 1], R[-1, 0], C[1, 0]), "x", 1)
    C[-1, 1] = shift(after(C[0, 1], C[1, 0], C[-1, 0]), "x", -1)

    R[3, 0] = shift(after(R[2, 0], C[-1, 0]), "z", 1)
    R[-3, 0] = shift(after(R[-2, 0], R[2, 0]), "z", -1)
    C[2, 0] = shift(after(C[1, 0], C[1, 1], R[-2, 0]), "x", 1)
    C[2, 1] = shift(after(C[-1, 1], C[1, 1]), "x", -1)

    far = shift(after(jnp.stack([R[3, 0], R[1, 1]]), C[-1, 1]), "z", 1)
    R[4, 0], R[2, 1] = (far, 0), (far, 1)
    R[-2, 1] = shift(after(R[-1, 1], R[-3, 0], R[3, 0]), "z", -1)
    R[-3, 1] = shift(after(R[-2, 1], C[2, 0], C[2, 1]), "z", -1)
    R[3, 1] = shift(far[1], "z", 1)
    R[4, 1] = shift(R[-3, 1], "z", -1)

    cols = [C[dx, dy] for dx in STEPS for dy in (0, 1)]
    own = [R[p] for p in GROUPS[0]]
    keep, send, cols = cross(scal, gate(own, R[3, 0], R[-3, 0])[0], cols, True)
    R[0, 1] = shift(after(row, keep, R[-3, 1]), "yh", 1)
    recv = shift(send, "c", 1)
    own, _ = gate([R[p] for p in GROUPS[1]], far, R[-3, 1])
    keep1, send1 = cross(scal, own, cols, False)
    recv1 = shift(send1, "c", 1)
    out = lags(scal, GROUPS[0], keep, recv, table, None)
    own, (out,) = gate([R[p] for p in GROUPS[2]], out)
    keep2, send2 = cross(scal, own, cols, False)
    recv2 = shift(send2, "c", 1)
    out = lags(scal, GROUPS[1], keep1, recv1, table, out)
    out = lags(scal, GROUPS[2], keep2, recv2, table, out)
    return out.reshape(N_Z * 20, COLS, LAGS)


def solution(mesh):
    fine = Mesh(mesh.devices.reshape(N_X, N_YL, N_Z, N_YH, N_C), ("x", "yl", "z", "yh", "c"))
    every = ("x", "yl", "z", "yh", "c")
    return jax.shard_map(
        shards,
        mesh=fine,
        in_specs=(P(every, None, None, None), P(every, None), P(every)),
        out_specs=P(("x", "yl"), ("z", "yh", "c"), None),
        check_vma=False,
    )
```
